256 devices in a mesh: hier: 16 (over x_hi, z), row: 16 (over x_lo, y, core).
Axes of the slice: x: 4 (x_hi: 2, x_lo: 2; x = x_hi * 2 + x_lo), y: 4, z: 8, core: 2. Of those that a mesh axis runs over, the one named last changes fastest.
Arguments:
- state: bfloat16 [48, 2, 1024, 1024], P('hier', None, 'row'), may hold values from -6 to 6
- prev_slope: float32 [48, 2, 1024, 1024], P('hier', None, 'row'), may hold values from -6 to 6
- accumulated: float32 [48, 2, 1024, 1024], P('hier', None, 'row'), may hold values from -6 to 6
- hamiltonian: bfloat16 [2, 1024, 1024], P(None, 'row'), as said below
- couple_v: float32 [6, 1024], replicated, may hold values from -4 to 4
- coupling: float32 [2, 6], replicated, may hold values from 0.2 to 1
- damping: float32 [6], replicated, may hold values from 0.2 to 2
- occupation: int32 [48, 6], P('hier'), may hold values from 0 to 3, as said below
- parents: int32 [48, 6], P('hier'), may hold values from -1 to 47, as said below
- children: int32 [48, 6], P('hier'), may hold values from -1 to 46, as said below
Outputs:
- slope: float32 [48, 2, 1024, 1024], P('hier', None, 'row')
- accumulated_out: float32 [48, 2, 1024, 1024], P('hier', None, 'row')
The draws below stay inside these ranges and needn't reach their ends.
Inputs may be any that keep to these rules, and one draw needn't show every extreme that they name: `occupation`: row s is the index of the operator in slot s. The rows are the 48 indices of smallest total among all indices of 6 entries with total at most 4, taken by total and then lexicographically; the all-zero index stands in the last slot, the others in a slot order drawn from the seed; the set is closed under lowering one entry. `parents`: entry (s, k) is the slot whose index equals slot s's index with entry k lowered by one, or -1 where entry k of slot s is 0. `children`: entry (s, k) is the slot whose index equals slot s's index with entry k raised by one, or -1 where that index is not among the 48. `hamiltonian`: Hermitian: the real part is symmetric, the imaginary part antisymmetric.
All inputs are finite; a program needn't handle non-finite values.
Results may differ from the reference program's by a relative error of at most 0.0029.
Values may be sent and summed in bfloat16 or wider, within the bound.
A program may use at most 192 MiB of HBM per device.

```python
import math
import jax
import jax.numpy as jnp
import numpy as np
from jax import lax

N = 1024
MODES = 6
ADOS = 48


def window_table():
    entries = [()]
    for mode in range(MODES):
        entries = [entry + (level,) for entry in entries for level in range(5)]
    chosen = [entry for entry in entries if sum(entry) <= 4]
    chosen = sorted(chosen, key=lambda entry: (sum(entry), entry))[:ADOS]
    lookup = {entry: place for place, entry in enumerate(chosen)}
    upward = np.full((ADOS, MODES), -1, np.int32)
    downward = np.full((ADOS, MODES), -1, np.int32)
    for place, entry in enumerate(chosen):
        for mode in range(MODES):
            raised = list(entry)
            raised[mode] = raised[mode] + 1
            upward[place, mode] = lookup.get(tuple(raised), -1)
            if entry[mode] > 0:
                lowered = list(entry)
                lowered[mode] = lowered[mode] - 1
                downward[place, mode] = lookup[tuple(lowered)]
    return (np.array(chosen, np.int32), upward, downward)


def hierarchy_draw(key):
    table, upward, downward = window_table()
    others = jax.random.permutation(jax.random.fold_in(key, 11), ADOS - 1).astype(jnp.int32)
    order = jnp.concatenate([jnp.array([ADOS - 1], jnp.int32), others])
    inverse = jnp.argsort(order)
    up_slots = jnp.where(upward >= 0, order[np.maximum(upward, 0)], -1).astype(jnp.int32)
    down_slots = jnp.where(downward >= 0, order[np.maximum(downward, 0)], -1).astype(jnp.int32)
    return (jnp.asarray(table)[inverse], down_slots[inverse], up_slots[inverse])


def draw_occupation(key, part):
    return hierarchy_draw(key)[0]


def draw_parents(key, part):
    return hierarchy_draw(key)[1]


def draw_children(key, part):
    return hierarchy_draw(key)[2]


def draw_hamiltonian(key, part):
    first_key, second_key = jax.random.split(jax.random.fold_in(key, 5))
    first = jax.random.normal(first_key, (N, N), jnp.float32)
    second = jax.random.normal(second_key, (N, N), jnp.float32)
    factor = (2.0 * N) ** (-0.5)
    real_part = (first + first.T) * factor
    imag_part = (second - second.T) * factor
    return jnp.stack([real_part, imag_part]).astype(jnp.bfloat16)


def block_levels(key, extent, shards, least, high):
    gain, own = 1.0, jax.random.fold_in(key, 6)
    for position, shards_of in shards:
        draws = jnp.exp(jax.random.uniform(jax.random.fold_in(own, position), (shards_of,), jnp.float32, least / len(shards), high / len(shards)))
        gain = gain * jnp.repeat(draws, extent[position] // shards_of).reshape([-1 if axis == position else 1 for axis in range(len(extent))])
    return gain


def centred(own_key, shape, scale, bound, shards=(), held_as=jnp.bfloat16):
    gain = block_levels(own_key, shape, shards, -0.22, 0.18) if shards else 1.0
    result = jax.random.normal(own_key, shape, jnp.float32) * scale * gain
    return jnp.minimum(jnp.maximum(result, -bound), bound).astype(held_as)


def setup_inputs(seed: int = 0) -> dict:
    key_of = jax.random.split(jax.random.key(seed), 11)
    state = centred(key_of[0], (ADOS, 2, N, N), 1.0, 6.0, ((0, 16), (2, 16)))
    prev_slope = centred(key_of[1], (ADOS, 2, N, N), 1.0, 6.0, ((0, 16), (2, 16)), jnp.float32)
    accumulated = centred(key_of[2], (ADOS, 2, N, N), 1.0, 6.0, ((0, 16), (2, 16)), jnp.float32)
    hamiltonian = draw_hamiltonian(jax.random.fold_in(key_of[10], 71), 0)
    couple_v = centred(key_of[4], (MODES, N), 1.0, 4.0, (), jnp.float32)
    coupling = jnp.clip(jax.random.uniform(key_of[5], (2, MODES), jnp.float32, 0.2, 1.0), 0.2, 1.0)
    damping = jnp.clip(jnp.exp(jax.random.uniform(key_of[6], (MODES,), jnp.float32, math.log(0.2), math.log(2.0))), 0.2, 2.0)
    occupation = draw_occupation(jax.random.fold_in(key_of[10], 71), 0)
    parents = draw_parents(jax.random.fold_in(key_of[10], 71), 0)
    children = draw_children(jax.random.fold_in(key_of[10], 71), 0)
    return {"state": state, "prev_slope": prev_slope, "accumulated": accumulated, "hamiltonian": hamiltonian, "couple_v": couple_v, "coupling": coupling, "damping": damping, "occupation": occupation, "parents": parents, "children": children}


step_size = 0.5


def complex_dot(left, right):
    real_part = jnp.dot(left[0], right[0], preferred_element_type=jnp.float32) - jnp.dot(left[1], right[1], preferred_element_type=jnp.float32)
    imag_part = jnp.dot(left[0], right[1], preferred_element_type=jnp.float32) + jnp.dot(left[1], right[0], preferred_element_type=jnp.float32)
    return real_part, imag_part


def reference(state, prev_slope, accumulated, hamiltonian, couple_v, coupling, damping, occupation, parents, children):
    section = (state.astype(jnp.float32) + 0.5 * step_size * prev_slope).astype(jnp.bfloat16)

    def single(index):
        operator = section[index]
        left_real, left_imag = complex_dot(hamiltonian, operator)
        right_real, right_imag = complex_dot(operator, hamiltonian)
        wide = operator.astype(jnp.float32)
        counts = occupation[index].astype(jnp.float32)
        decay = jnp.sum(counts * damping)
        out_real = (left_imag - right_imag) - decay * wide[0]
        out_imag = -(left_real - right_real) - decay * wide[1]
        for mode in range(MODES):
            vrows = couple_v[mode][:, None]
            vcols = couple_v[mode][None, :]
            diff = vrows - vcols
            total = vrows + vcols
            child = children[index, mode]
            keep_up = (child >= 0).astype(jnp.float32)
            upper = section[jnp.maximum(child, 0)].astype(jnp.float32) * keep_up
            out_real = out_real + diff * upper[1]
            out_imag = out_imag - diff * upper[0]
            parent = parents[index, mode]
            keep_down = (parent >= 0).astype(jnp.float32)
            lower = section[jnp.maximum(parent, 0)].astype(jnp.float32) * (keep_down * counts[mode])
            g_real = coupling[0, mode] * diff
            g_imag = coupling[1, mode] * total
            prod_real = g_real * lower[0] - g_imag * lower[1]
            prod_imag = g_real * lower[1] + g_imag * lower[0]
            out_real = out_real + prod_imag
            out_imag = out_imag - prod_real
        return jnp.stack([out_real, out_imag])

    slope = lax.map(single, jnp.arange(ADOS, dtype=jnp.int32))
    return slope, accumulated + (step_size / 3.0) * slope
```

```python
import jax
import jax.numpy as jnp
import numpy as np
from jax import lax
from jax.experimental import pallas as pl
from jax.experimental.pallas import tpu as pltpu
from jax.sharding import PartitionSpec as P

MESH = pl.DeviceIdType.MESH
N = 1024
MODES = 6
ADOS = 48
STEP = 0.5
F32 = jnp.float32
BF16 = jnp.bfloat16


def window_table():
    entries = [()]
    for _ in range(MODES):
        entries = [entry + (level,) for entry in entries for level in range(5)]
    chosen = [entry for entry in entries if sum(entry) <= 4]
    return sorted(chosen, key=lambda entry: (sum(entry), entry))[:ADOS]


TABLE = window_table()
PLACE = {entry: place for place, entry in enumerate(TABLE)}


def key_of(entry):
    return sum(entry[k] * 5**k for k in range(MODES))


def shifted(entry, mode, by):
    return PLACE.get(entry[:mode] + (entry[mode] + by,) + entry[mode + 1 :])


def key_table():
    keys = np.full((8, 128), -1, np.int32)
    keys[:, :ADOS] = [key_of(entry) for entry in TABLE]
    return keys


R_HN = 0
R_HU = 1
R_HD = 3
R_H2 = 5
R_HP = 7
R_L = 15
R_LP = 23
R_LR = 31
R_XR = 39
R_X = 41
R_Z = 43
R_ZX = 51
R_M = 59
R_C = 75
R_CX = 83
R_CR = 91
R_CF = 93
N_RECV = 95
N_SEND = 110


def kernel(
    state,
    prev,
    ham,
    cv,
    coup,
    damp,
    occ,
    tab,
    slope,
    st_v,
    pv_v,
    sblk,
    amat,
    hn,
    lb,
    lout,
    lret,
    zin,
    xin,
    xrp,
    xrm,
    ccan,
    cout,
    cx,
    crp,
    crm,
    cret,
    rbuf,
    meta_out,
    meta_in,
    meta_v,
    meta_s,
    vt,
    dk,
    dg,
    eg,
    lsem,
    ssem,
    rsem,
):
    h = lax.axis_index("hier")
    r = lax.axis_index("row")
    xh, z = lax.div(h, 8), lax.rem(h, 8)
    p, c = lax.div(r, 2), lax.rem(r, 2)
    xl, y = lax.div(p, 4), lax.rem(p, 4)
    oc = 1 - c

    def chip(dx, dy):
        return lax.rem(xl + dx, 2) * 4 + lax.rem(y + dy, 4)

    def zrow(dz):
        return lax.rem(z + dz, 8)

    def rowdev(dx, dy):
        return (h, chip(dx, dy) * 2 + c)

    def zdev(dz):
        return (xh * 8 + zrow(dz), r)

    other_core = (h, p * 2 + oc)
    other_row = ((1 - xl) * 4 + y) * 2 + c
    xhp = lax.rem(xh + xl, 2)
    xhm = lax.rem(xh + 1 - xl, 2)
    x_up = (xhp * 8 + z, other_row)
    x_down = (xhm * 8 + z, other_row)
    x_cross = ((1 - xh) * 8 + z, other_row)
    h2 = (1 - xh) * 8 + z

    row_offsets = [(dx, dy) for dy in (1, 3, 0, 2) for dx in (0, 1) if dx or dy]
    z_offsets = [4, 3, 5, 2, 6, 1, 7]

    cp_h = pltpu.make_async_copy(ham, hn.at[:, p, c], lsem.at[0])
    cp_s = pltpu.make_async_copy(state, st_v, lsem.at[1])
    cp_p = pltpu.make_async_copy(prev, pv_v, lsem.at[2])
    cp_h.start()
    cp_s.start()
    cp_p.start()

    barrier = pltpu.get_barrier_semaphore()
    greeted = [rowdev(dx, dy) for dx, dy in row_offsets]
    greeted += [other_core, x_cross]
    greeted += [(lax.rem(h + d, 16), r) for d in range(1, 16)]
    for dev in greeted:
        pl.semaphore_signal(barrier, inc=1, device_id=dev, device_id_type=MESH)

    lane = lax.broadcasted_iota(jnp.int32, (8, 128), 1)
    line = lax.broadcasted_iota(jnp.int32, (8, 128), 0)
    slots = jnp.zeros((8, 128), jnp.int32)
    places = jnp.zeros((8, 128), jnp.int32)
    for j in range(3):
        key = occ[j, 0]
        for k in range(1, MODES):
            key = key + occ[j, k] * (5**k)
        hit = tab[...] == key
        slots = slots + jnp.where(hit, 3 * h + j, 0)
        place = jnp.sum(jnp.where(hit, lane, 0), axis=1, keepdims=True)
        places = places + jnp.where(lane == 3 * h + j, place, 0)
    mine = jnp.where(line == 0, slots, places)
    meta_out[...] = mine

    pl.semaphore_wait(barrier, len(greeted))

    sent = []

    def send(src, dst, to, dev):
        copy = pltpu.make_async_remote_copy(
            src_ref=src,
            dst_ref=dst,
            send_sem=ssem.at[len(sent)],
            recv_sem=rsem.at[to],
            device_id=dev,
            device_id_type=MESH,
        )
        copy.start()
        sent.append(copy)

    def arrived(dst, to):
        pltpu.make_async_remote_copy(
            src_ref=dst,
            dst_ref=dst,
            send_sem=ssem.at[0],
            recv_sem=rsem.at[to],
            device_id=other_core,
            device_id_type=MESH,
        ).wait_recv()

    def hblk(q):
        return hn.at[:, q, c]

    def send_h(q, to, dev):
        send(hblk(q), hblk(q), to, dev)

    cp_h.wait()
    send_h(p, R_HN, x_cross)
    send_h(p, R_HU, rowdev(0, 1))
    send_h(p, R_HD, rowdev(0, 3))
    send_h(p, R_HP, other_core)

    cp_s.wait()
    cp_p.wait()

    @pl.loop(0, 3)
    def _(a):
        for half in range(2):
            rows = pl.ds(32 * half, 32)
            for b in range(8):
                cols = pl.ds(128 * b, 128)
                parts = []
                for ri in range(2):
                    value = st_v[a, ri, rows, cols].astype(F32) + (0.5 * STEP) * pv_v[a, ri, rows, cols]
                    parts.append(value.astype(BF16))
                    sblk[b, half, a, ri] = parts[ri]
                    amat[half, a, ri, :, cols] = parts[ri]
                late = pl.ds(N + 128 * b, 128)
                amat[half, a, 0, :, late] = -parts[1]
                amat[half, a, 1, :, late] = parts[0]

    send(sblk.at[pl.ds(0, 4), 1 - xh], xrp, R_XR, x_up)
    send(sblk.at[pl.ds(4, 4), 1 - xh], xrm, R_XR + 1, x_down)
    for dz in z_offsets:
        send(sblk.at[zrow(dz), xh], zin.at[pl.ds(3 * h, 3)], R_Z + dz, zdev(dz))
    for dx, dy in row_offsets:
        q = chip(dx, dy)
        send(sblk.at[q], lb.at[p, c], R_L + 4 * dx + dy, (h, q * 2 + c))
    send(sblk.at[p], lb.at[p, c], R_LP, other_core)
    for d in range(1, 16):
        send(meta_out, meta_in.at[h], R_M + d, (lax.rem(h + d, 16), r))
    meta_in[h] = mine
    lb[p, c] = sblk[p]
    zin[pl.ds(3 * h, 3)] = sblk[z, xh]

    arrived(xrp, R_XR)
    send(xrp, xin.at[pl.ds(0, 4)], R_X, x_up)
    arrived(xrm, R_XR + 1)
    send(xrm, xin.at[pl.ds(4, 4)], R_X + 1, x_down)

    q = chip(1, 0)
    arrived(hblk(q), R_HN)
    send_h(q, R_HU + 1, rowdev(0, 1))
    send_h(q, R_HD + 1, rowdev(0, 3))
    send_h(q, R_HP + 4, other_core)

    for k in range(MODES):
        line_v = cv[pl.ds(k, 1), pl.ds(pl.multiple_of(128 * p, 128), 128)]
        vt[k] = jnp.broadcast_to(line_v, (128, 128)).T
        v_rows = vt[k, pl.ds(pl.multiple_of(64 * c + 32 * xh, 32), 32), :]
        v_cols = cv[pl.ds(k, 1), pl.ds(pl.multiple_of(128 * z, 128), 128)]
        diff = v_rows - v_cols
        dk[k] = diff
        dg[k] = coup[0, k] * diff
        eg[k] = coup[1, k] * (v_rows + v_cols)

    arrived(xin.at[pl.ds(0, 4)], R_X)
    arrived(xin.at[pl.ds(4, 4)], R_X + 1)
    for dz in z_offsets:
        send(xin.at[zrow(dz)], zin.at[pl.ds(3 * h2, 3)], R_ZX + dz, zdev(dz))
    zin[pl.ds(3 * h2, 3)] = xin[z]

    for dx, dy in row_offsets:
        back = (4 - dy) % 4
        q = chip(dx, back)
        arrived(lb.at[q, c], R_L + 4 * dx + dy)
        send(lb.at[q, c], lb.at[q, c], R_LP + 4 * dx + back, other_core)

    for dx in range(2):
        arrived(hblk(chip(dx, 3)), R_HU + dx)
        send_h(chip(dx, 3), R_HP + 4 * dx + 3, other_core)
        arrived(hblk(chip(dx, 1)), R_HD + dx)
        send_h(chip(dx, 1), R_HP + 4 * dx + 1, other_core)
    send_h(lax.rem(y + 3, 4), R_H2, rowdev(0, 1))
    send_h(4 + lax.rem(y + 1, 4), R_H2 + 1, rowdev(0, 3))

    for d in range(1, 16):
        arrived(meta_in.at[lax.rem(h + 16 - d, 16)], R_M + d)
    meta_v[...] = jnp.minimum(jnp.sum(meta_in[...], axis=0), ADOS - 1)
    cp_m = pltpu.make_async_copy(meta_v, meta_s, lsem.at[3])
    cp_m.start()
    for dz in z_offsets:
        zs = zrow(8 - dz)
        arrived(zin.at[pl.ds(3 * (xh * 8 + zs), 3)], R_Z + dz)
        arrived(zin.at[pl.ds(3 * ((1 - xh) * 8 + zs), 3)], R_ZX + dz)
    cp_m.wait()
    for place, entry in enumerate(TABLE):
        re = jnp.zeros((32, 128), F32)
        im = jnp.zeros((32, 128), F32)
        for k in range(MODES):
            child = shifted(entry, k, 1)
            if child is not None:
                near = zin[meta_s[0, child]].astype(F32)
                re = re + dk[k] * near[1]
                im = im - dk[k] * near[0]
            if entry[k] > 0:
                near = zin[meta_s[0, shifted(entry, k, -1)]].astype(F32)
                add_re = dg[k] * near[1] + eg[k] * near[0]
                add_im = eg[k] * near[1] - dg[k] * near[0]
                if entry[k] > 1:
                    add_re = add_re * float(entry[k])
                    add_im = add_im * float(entry[k])
                re = re + add_re
                im = im + add_im
        ccan[place, 0] = re.astype(BF16)
        ccan[place, 1] = im.astype(BF16)
    for slot in range(ADOS):
        cout[slot] = ccan[meta_s[1, slot]]
    for dz in z_offsets:
        send(cout.at[pl.ds(3 * ((1 - xh) * 8 + zrow(dz)), 3)], cx.at[z], R_CX + dz, zdev(dz))
    for dz in z_offsets:
        send(cout.at[pl.ds(3 * (xh * 8 + zrow(dz)), 3)], cret.at[xh, z], R_C + dz, zdev(dz))
    cx[z] = cout[pl.ds(3 * h2, 3)]
    cret[xh, z] = cout[pl.ds(3 * h, 3)]

    arrived(hblk(lax.rem(y + 2, 4)), R_H2)
    send_h(lax.rem(y + 2, 4), R_HP + 2, other_core)
    arrived(hblk(4 + lax.rem(y + 2, 4)), R_H2 + 1)
    send_h(4 + lax.rem(y + 2, 4), R_HP + 6, other_core)
    for dx in range(2):
        for dy in range(4):
            arrived(lb.at[chip(dx, dy), oc], R_LP + 4 * dx + dy)

    @pl.loop(0, 3)
    def _(a):
        real = lb[:, :, :, a, 0].reshape(N, 128)
        imag = lb[:, :, :, a, 1].reshape(N, 128)
        rhs = jnp.concatenate(
            [jnp.concatenate([real, imag], 1), jnp.concatenate([-imag, real], 1)], 0
        )
        for m in range(2):
            lhs = jnp.concatenate(
                [hn[ri, pl.ds(4 * m, 4), c].reshape(256, N) for ri in range(2)], 1
            )
            out = jnp.dot(lhs, rhs, preferred_element_type=F32).astype(BF16)
            out = out.reshape(4, 2, 32, 256)
            lout[pl.ds(4 * m, 4), :, a, 0] = out[..., :128]
            lout[pl.ds(4 * m, 4), :, a, 1] = out[..., 128:]

    for dx, dy in row_offsets:
        q = chip(dx, dy)
        send(lout.at[q], lret.at[p], R_LR + 4 * dx + dy, (h, q * 2 + c))
    lret[p] = lout[p]

    for dx in range(2):
        for dy in range(4):
            if dy == 2:
                q = 4 * dx + lax.rem(y + 2, 4)
            else:
                q = chip(dx, dy)
            arrived(hn.at[:, q, oc], R_HP + 4 * dx + dy)

    @pl.loop(0, 4)
    def _(n):
        cols = pl.ds(pl.multiple_of(256 * n, 256), 256)
        rhs = jnp.concatenate(
            [hn[ri, :, :, :, cols].reshape(N, 256) for ri in range(2)], 0
        )
        lhs = amat[...].reshape(384, 2 * N)
        out = jnp.dot(lhs, rhs, preferred_element_type=F32)
        rbuf[:, :, :, :, cols] = out.reshape(2, 3, 2, 32, 256)

    for dz in z_offsets:
        arrived(cx.at[zrow(8 - dz)], R_CX + dz)
    send(cx.at[pl.ds(0, 4)], crp, R_CR, x_up)
    send(cx.at[pl.ds(4, 4)], crm, R_CR + 1, x_down)
    arrived(crp, R_CR)
    send(crp, cret.at[1 - xhp, pl.ds(0, 4)], R_CF, x_up)
    arrived(crm, R_CR + 1)
    send(crm, cret.at[1 - xhm, pl.ds(4, 4)], R_CF + 1, x_down)

    for dx, dy in row_offsets:
        back = (4 - dy) % 4
        arrived(lret.at[chip(dx, back)], R_LR + 4 * dx + dy)
    for dz in z_offsets:
        arrived(cret.at[xh, zrow(8 - dz)], R_C + dz)
    arrived(cret.at[1 - xh, pl.ds(0, 4)], R_CF)
    arrived(cret.at[1 - xh, pl.ds(4, 4)], R_CF + 1)

    @pl.loop(0, 3)
    def _(a):
        decay = occ[a, 0].astype(F32) * damp[0]
        for k in range(1, MODES):
            decay = decay + occ[a, k].astype(F32) * damp[k]
        for half in range(2):
            for b in range(8):
                cols = pl.ds(128 * b, 128)
                for ri in range(2):
                    turned = lret[b, half, a, 1 - ri].astype(F32) - rbuf[half, a, 1 - ri, :, cols]
                    if ri:
                        turned = -turned
                    value = turned - decay * sblk[b, half, a, ri].astype(F32)
                    value = value + cret[half, b, a, ri].astype(F32)
                    slope[a, ri, pl.ds(32 * half, 32), cols] = value

    for copy in sent:
        copy.wait_send()


def shards(state, prev_slope, accumulated, hamiltonian, couple_v, coupling, damping, occupation, parents, children):
    vmem = pltpu.VMEM
    anywhere = pl.BlockSpec(memory_space=pl.ANY)
    in_vmem = pl.BlockSpec(memory_space=pltpu.VMEM)
    in_smem = pl.BlockSpec(memory_space=pltpu.SMEM)
    slope = pl.pallas_call(
        kernel,
        name="section",
        out_shape=jax.ShapeDtypeStruct((3, 2, 64, N), F32),
        in_specs=[anywhere, anywhere, anywhere, in_vmem, in_smem, in_smem, in_smem, in_vmem],
        out_specs=in_vmem,
        scratch_shapes=[
            vmem((3, 2, 64, N), BF16),
            vmem((3, 2, 64, N), F32),
            vmem((8, 2, 3, 2, 32, 128), BF16),
            vmem((2, 3, 2, 32, 2 * N), BF16),
            vmem((2, 8, 2, 64, N), BF16),
            vmem((8, 2, 2, 3, 2, 32, 128), BF16),
            vmem((8, 2, 3, 2, 32, 128), BF16),
            vmem((8, 2, 3, 2, 32, 128), BF16),
            vmem((ADOS, 2, 32, 128), BF16),
            vmem((8, 3, 2, 32, 128), BF16),
            vmem((4, 3, 2, 32, 128), BF16),
            vmem((4, 3, 2, 32, 128), BF16),
            vmem((ADOS, 2, 32, 128), BF16),
            vmem((ADOS, 2, 32, 128), BF16),
            vmem((8, 3, 2, 32, 128), BF16),
            vmem((4, 3, 2, 32, 128), BF16),
            vmem((4, 3, 2, 32, 128), BF16),
            vmem((2, 8, 3, 2, 32, 128), BF16),
            vmem((2, 3, 2, 32, N), F32),
            vmem((8, 128), jnp.int32),
            vmem((16, 8, 128), jnp.int32),
            vmem((8, 128), jnp.int32),
            pltpu.SMEM((8, 128), jnp.int32),
            vmem((MODES, 128, 128), F32),
            vmem((MODES, 32, 128), F32),
            vmem((MODES, 32, 128), F32),
            vmem((MODES, 32, 128), F32),
            pltpu.SemaphoreType.DMA((4,)),
            pltpu.SemaphoreType.DMA((N_SEND,)),
            pltpu.SemaphoreType.DMA((N_RECV,)),
        ],
        compiler_params=pltpu.CompilerParams(collective_id=0, has_side_effects=True),
    )(state, prev_slope, hamiltonian, couple_v, coupling, damping, occupation, jnp.asarray(key_table()))
    return slope, accumulated + (STEP / 3.0) * slope


def solution(mesh):
    block = P("hier", None, "row", None)
    return jax.shard_map(
        shards,
        mesh=mesh,
        in_specs=(
            block,
            block,
            block,
            P(None, "row", None),
            P(),
            P(),
            P(),
            P("hier", None),
            P("hier", None),
            P("hier", None),
        ),
        out_specs=(block, block),
        check_vma=False,
    )
```

```python
import jax
import jax.numpy as jnp
import numpy as np
from jax import lax
from jax.experimental import pallas as pl
from jax.experimental.pallas import tpu as pltpu
from jax.sharding import PartitionSpec as P

MESH = pl.DeviceIdType.MESH
N = 1024
MODES = 6
ADOS = 48
STEP = 0.5
F32 = jnp.float32
BF16 = jnp.bfloat16


def window_table():
    entries = [()]
    for _ in range(MODES):
        entries = [entry + (level,) for entry in entries for level in range(5)]
    chosen = [entry for entry in entries if sum(entry) <= 4]
    return sorted(chosen, key=lambda entry: (sum(entry), entry))[:ADOS]


TABLE = window_table()
PLACE = {entry: place for place, entry in enumerate(TABLE)}


def key_of(entry):
    return sum(entry[k] * 5**k for k in range(MODES))


def shifted(entry, mode, by):
    return PLACE.get(entry[:mode] + (entry[mode] + by,) + entry[mode + 1 :])


def key_table():
    keys = np.full((8, 128), -1, np.int32)
    keys[:, :ADOS] = [key_of(entry) for entry in TABLE]
    return keys


R_HN = 0
R_HU = 1
R_HD = 3
R_H2 = 5
R_HP = 9
R_L = 17
R_LP = 25
R_LR = 33
R_M = 41
R_A = 57
R_C = 89
N_RECV = 121
N_SEND = 140


def kernel(
    state,
    prev,
    acc,
    ham,
    cv_in,
    coup_in,
    damp_in,
    occ_in,
    tab_in,
    slope,
    acc_out,
    st_v,
    pv_v,
    acc_v,
    cv,
    tab,
    coup,
    damp,
    occ,
    sblk,
    amat,
    hn,
    lb,
    lout,
    lret,
    zin_0,
    zin_1,
    ccan,
    cout,
    cret,
    rbuf,
    slope_v,
    meta_out,
    meta_in,
    meta_v,
    meta_s,
    vt,
    dk,
    dg,
    eg,
    lsem,
    ssem,
    rsem,
):
    h = lax.axis_index("hier")
    r = lax.axis_index("row")
    xh, z = lax.div(h, 8), lax.rem(h, 8)
    p, c = lax.div(r, 2), lax.rem(r, 2)
    xl, y = lax.div(p, 4), lax.rem(p, 4)
    oc = 1 - c
    zin = (zin_0, zin_1)

    def chip(dx, dy):
        return lax.rem(xl + dx, 2) * 4 + lax.rem(y + dy, 4)

    def rowdev(dx, dy):
        return (h, chip(dx, dy) * 2 + c)

    def hier(dx, dz):
        return lax.rem(xh + dx, 2), lax.rem(z + dz, 8)

    other_core = (h, p * 2 + oc)
    x_cross = ((1 - xh) * 8 + z, ((1 - xl) * 4 + y) * 2 + c)

    row_offsets = [(dx, dy) for dy in (2, 1, 3, 0) for dx in (1, 0) if dx or dy]
    hier_offsets = [(dx, dz) for dz in (4, 3, 5, 2, 6, 1, 7, 0) for dx in (1, 0) if dx or dz]

    cp_h = pltpu.make_async_copy(ham, hn.at[:, p, c], lsem.at[0])
    cp_s = pltpu.make_async_copy(state, st_v, lsem.at[1])
    cp_p = pltpu.make_async_copy(prev, pv_v, lsem.at[2])
    cp_s.start()
    cp_p.start()
    cp_h.start()
    small = []
    for i, (src, dst) in enumerate(
        [(occ_in, occ), (tab_in, tab), (cv_in, cv), (coup_in, coup), (damp_in, damp), (acc, acc_v)]
    ):
        small.append(pltpu.make_async_copy(src, dst, lsem.at[10 + i]))
        small[i].start()

    barrier = pltpu.get_barrier_semaphore()
    greeted = []
    for dx, dz in hier_offsets:
        hx, hz = hier(dx, dz)
        greeted.append((hx * 8 + hz, r))
    greeted += [rowdev(dx, dy) for dx, dy in row_offsets]
    greeted += [x_cross, other_core]
    for dev in greeted:
        pl.semaphore_signal(barrier, inc=1, device_id=dev, device_id_type=MESH)

    for copy in small[:2]:
        copy.wait()
    lane = lax.broadcasted_iota(jnp.int32, (8, 128), 1)
    line = lax.broadcasted_iota(jnp.int32, (8, 128), 0)
    slots = jnp.zeros((8, 128), jnp.int32)
    places = jnp.zeros((8, 128), jnp.int32)
    for j in range(3):
        key = occ[j, 0]
        for k in range(1, MODES):
            key = key + occ[j, k] * (5**k)
        hit = tab[...] == key
        slots = slots + jnp.where(hit, 3 * h + j, 0)
        place = jnp.sum(jnp.where(hit, lane, 0), axis=1, keepdims=True)
        places = places + jnp.where(lane == 3 * h + j, place, 0)
    mine = jnp.where(line == 0, slots, places)
    meta_out[...] = mine
    meta_in[h] = mine

    cp_s.wait()
    cp_p.wait()

    @pl.loop(0, 3)
    def _(a):
        for quarter in range(4):
            rows = pl.ds(16 * quarter, 16)
            for b in range(8):
                cols = pl.ds(128 * b, 128)
                parts = []
                for ri in range(2):
                    value = st_v[a, ri, rows, cols].astype(F32) + (0.5 * STEP) * pv_v[a, ri, rows, cols]
                    parts.append(value.astype(BF16))
                    sblk[b, quarter, a, ri] = parts[ri]
                    amat[quarter, a, ri, :, cols] = parts[ri]
                late = pl.ds(N + 128 * b, 128)
                amat[quarter, a, 0, :, late] = -parts[1]
                amat[quarter, a, 1, :, late] = parts[0]

    cp_h.wait()
    pl.semaphore_wait(barrier, len(greeted))

    sent = []

    def send(src, dst, to, dev):
        copy = pltpu.make_async_remote_copy(
            src_ref=src,
            dst_ref=dst,
            send_sem=ssem.at[len(sent)],
            recv_sem=rsem.at[to],
            device_id=dev,
            device_id_type=MESH,
        )
        copy.start()
        sent.append(copy)

    def arrived(dst, to):
        pltpu.make_async_remote_copy(
            src_ref=dst,
            dst_ref=dst,
            send_sem=ssem.at[0],
            recv_sem=rsem.at[to],
            device_id=other_core,
            device_id_type=MESH,
        ).wait_recv()

    def hblk(q):
        return hn.at[:, q, c]

    def send_h(q, to, dev):
        send(hblk(q), hblk(q), to, dev)

    send_h(p, R_HN, x_cross)
    send_h(p, R_HU, rowdev(0, 1))
    send_h(p, R_HD, rowdev(0, 3))
    for q in range(2):
        for dx, dz in hier_offsets:
            hx, hz = hier(dx, dz)
            dev = (hx * 8 + hz, r)
            if q == 0:
                send(meta_out, meta_in.at[h], R_M + 8 * dx + dz, dev)
            send(sblk.at[hz, 2 * hx + q], zin[q].at[pl.ds(3 * h, 3)], R_A + 16 * q + 8 * dx + dz, dev)
    for dx, dy in row_offsets:
        q = chip(dx, dy)
        send(sblk.at[q], lb.at[p, c], R_L + 4 * dx + dy, (h, q * 2 + c))
    send_h(p, R_HP, other_core)
    send(sblk.at[p], lb.at[p, c], R_LP, other_core)
    lb[p, c] = sblk[p]
    for q in range(2):
        zin[q][pl.ds(3 * h, 3)] = sblk[z, 2 * xh + q]

    for copy in small[2:]:
        copy.wait()
    for k in range(MODES):
        line_v = cv[pl.ds(k, 1), pl.ds(pl.multiple_of(128 * p, 128), 128)]
        vt[k] = jnp.broadcast_to(line_v, (128, 128)).T
        v_rows = vt[k, pl.ds(pl.multiple_of(64 * c + 32 * xh, 32), 32), :]
        v_cols = cv[pl.ds(k, 1), pl.ds(pl.multiple_of(128 * z, 128), 128)]
        diff = v_rows - v_cols
        dk[k] = diff
        dg[k] = coup[0, k] * diff
        eg[k] = coup[1, k] * (v_rows + v_cols)

    q = chip(1, 0)
    arrived(hblk(q), R_HN)
    send_h(q, R_HU + 1, rowdev(0, 1))
    send_h(q, R_HD + 1, rowdev(0, 3))
    send_h(q, R_HP + 4, other_core)

    def pass_on_h(dx):
        below, above = chip(dx, 3), chip(dx, 1)
        arrived(hblk(below), R_HU + dx)
        send(hn.at[0, below, c], hn.at[0, below, c], R_H2 + 2 * dx, rowdev(0, 1))
        arrived(hblk(above), R_HD + dx)
        send(hn.at[1, above, c], hn.at[1, above, c], R_H2 + 2 * dx + 1, rowdev(0, 3))
        send_h(below, R_HP + 4 * dx + 3, other_core)
        send_h(above, R_HP + 4 * dx + 1, other_core)

    pass_on_h(0)

    for dx, dz in hier_offsets:
        hx, hz = hier(dx, 8 - dz)
        arrived(meta_in.at[hx * 8 + hz], R_M + 8 * dx + dz)
    meta_v[...] = jnp.minimum(jnp.sum(meta_in[...], axis=0), ADOS - 1)
    cp_m = pltpu.make_async_copy(meta_v, meta_s, lsem.at[3])
    cp_m.start()
    cp_m.wait()

    def couple(q):
        for dx, dz in hier_offsets:
            hx, hz = hier(dx, 8 - dz)
            arrived(zin[q].at[pl.ds(3 * (hx * 8 + hz), 3)], R_A + 16 * q + 8 * dx + dz)
        rows = pl.ds(16 * q, 16)
        for place, entry in enumerate(TABLE):
            re = jnp.zeros((16, 128), F32)
            im = jnp.zeros((16, 128), F32)
            for k in range(MODES):
                child = shifted(entry, k, 1)
                if child is not None:
                    near = zin[q][meta_s[0, child]].astype(F32)
                    re = re + dk[k, rows] * near[1]
                    im = im - dk[k, rows] * near[0]
                if entry[k] > 0:
                    near = zin[q][meta_s[0, shifted(entry, k, -1)]].astype(F32)
                    add_re = dg[k, rows] * near[1] + eg[k, rows] * near[0]
                    add_im = eg[k, rows] * near[1] - dg[k, rows] * near[0]
                    if entry[k] > 1:
                        add_re = add_re * float(entry[k])
                        add_im = add_im * float(entry[k])
                    re = re + add_re
                    im = im + add_im
            ccan[place, 0] = re.astype(BF16)
            ccan[place, 1] = im.astype(BF16)
        for slot in range(ADOS):
            cout[q, slot] = ccan[meta_s[1, slot]]
        for dx, dz in hier_offsets:
            hx, hz = hier(dx, dz)
            to = hx * 8 + hz
            send(cout.at[q, pl.ds(3 * to, 3)], cret.at[2 * xh + q, z], R_C + 16 * q + 8 * dx + dz, (to, r))
        cret[2 * xh + q, z] = cout[q, pl.ds(3 * h, 3)]

    pass_on_h(1)
    couple(0)

    for dx, dy in row_offsets[2:] + row_offsets[:2]:
        back = (4 - dy) % 4
        q = chip(dx, back)
        arrived(lb.at[q, c], R_L + 4 * dx + dy)
        send(lb.at[q, c], lb.at[q, c], R_LP + 4 * dx + back, other_core)
    for dx in range(2):
        q = chip(dx, 2)
        arrived(hn.at[0, q, c], R_H2 + 2 * dx)
        arrived(hn.at[1, q, c], R_H2 + 2 * dx + 1)
        send_h(q, R_HP + 4 * dx + 2, other_core)

    couple(1)

    for dx in range(2):
        for dy in range(4):
            arrived(lb.at[chip(dx, dy), oc], R_LP + 4 * dx + dy)

    @pl.loop(0, 3)
    def _(a):
        real = lb[:, :, :, a, 0].reshape(N, 128)
        imag = lb[:, :, :, a, 1].reshape(N, 128)
        rhs = jnp.concatenate(
            [jnp.concatenate([real, imag], 1), jnp.concatenate([-imag, real], 1)], 0
        )
        for m in range(2):
            lhs = jnp.concatenate(
                [hn[ri, pl.ds(4 * m, 4), c].reshape(256, N) for ri in range(2)], 1
            )
            out = jnp.dot(lhs, rhs, preferred_element_type=F32).astype(BF16)
            out = out.reshape(4, 4, 16, 256)
            lout[pl.ds(4 * m, 4), :, a, 0] = out[..., :128]
            lout[pl.ds(4 * m, 4), :, a, 1] = out[..., 128:]

    for dx, dy in row_offsets:
        q = chip(dx, dy)
        send(lout.at[q], lret.at[p], R_LR + 4 * dx + dy, (h, q * 2 + c))
    lret[p] = lout[p]

    for dx in range(2):
        for dy in range(4):
            arrived(hn.at[:, chip(dx, dy), oc], R_HP + 4 * dx + dy)

    @pl.loop(0, 4)
    def _(n):
        cols = pl.ds(pl.multiple_of(256 * n, 256), 256)
        rhs = jnp.concatenate(
            [hn[ri, :, :, :, cols].reshape(N, 256) for ri in range(2)], 0
        )
        lhs = amat[...].reshape(384, 2 * N)
        out = jnp.dot(lhs, rhs, preferred_element_type=F32)
        rbuf[:, :, :, :, cols] = out.reshape(4, 3, 2, 16, 256)

    for q in range(2):
        for dx, dz in hier_offsets:
            hx, hz = hier(dx, 8 - dz)
            arrived(cret.at[2 * hx + q, hz], R_C + 16 * q + 8 * dx + dz)
    for dx, dy in row_offsets:
        back = (4 - dy) % 4
        arrived(lret.at[chip(dx, back)], R_LR + 4 * dx + dy)

    @pl.loop(0, 3)
    def _(a):
        decay = occ[a, 0].astype(F32) * damp[0]
        for k in range(1, MODES):
            decay = decay + occ[a, k].astype(F32) * damp[k]
        for quarter in range(4):
            for b in range(8):
                cols = pl.ds(128 * b, 128)
                for ri in range(2):
                    turned = lret[b, quarter, a, 1 - ri].astype(F32) - rbuf[quarter, a, 1 - ri, :, cols]
                    if ri:
                        turned = -turned
                    value = turned - decay * sblk[b, quarter, a, ri].astype(F32)
                    value = value + cret[quarter, b, a, ri].astype(F32)
                    rows = pl.ds(16 * quarter, 16)
                    slope_v[a, ri, rows, cols] = value
                    pv_v[a, ri, rows, cols] = acc_v[a, ri, rows, cols] + (STEP / 3.0) * value
        pltpu.make_async_copy(slope_v.at[a], slope.at[a], lsem.at[4 + a]).start()
        pltpu.make_async_copy(pv_v.at[a], acc_out.at[a], lsem.at[7 + a]).start()

    for a in range(3):
        pltpu.make_async_copy(slope_v.at[a], slope.at[a], lsem.at[4 + a]).wait()
        pltpu.make_async_copy(pv_v.at[a], acc_out.at[a], lsem.at[7 + a]).wait()
    for copy in sent:
        copy.wait_send()


def shards(state, prev_slope, accumulated, hamiltonian, couple_v, coupling, damping, occupation, parents, children):
    vmem = pltpu.VMEM
    anywhere = pl.BlockSpec(memory_space=pl.ANY)
    block = jax.ShapeDtypeStruct((3, 2, 64, N), F32)
    return pl.pallas_call(
        kernel,
        name="section",
        out_shape=(block, block),
        in_specs=[anywhere] * 9,
        out_specs=(anywhere, anywhere),
        scratch_shapes=[
            vmem((3, 2, 64, N), BF16),
            vmem((3, 2, 64, N), F32),
            vmem((3, 2, 64, N), F32),
            vmem((MODES, N), F32),
            vmem((8, 128), jnp.int32),
            pltpu.SMEM((2, MODES), F32),
            pltpu.SMEM((MODES,), F32),
            pltpu.SMEM((3, MODES), jnp.int32),
            vmem((8, 4, 3, 2, 16, 128), BF16),
            vmem((4, 3, 2, 16, 2 * N), BF16),
            vmem((2, 8, 2, 64, N), BF16),
            vmem((8, 2, 4, 3, 2, 16, 128), BF16),
            vmem((8, 4, 3, 2, 16, 128), BF16),
            vmem((8, 4, 3, 2, 16, 128), BF16),
            vmem((ADOS, 2, 16, 128), BF16),
            vmem((ADOS, 2, 16, 128), BF16),
            vmem((ADOS, 2, 16, 128), BF16),
            vmem((2, ADOS, 2, 16, 128), BF16),
            vmem((4, 8, 3, 2, 16, 128), BF16),
            vmem((4, 3, 2, 16, N), F32),
            vmem((3, 2, 64, N), F32),
            vmem((8, 128), jnp.int32),
            vmem((16, 8, 128), jnp.int32),
            vmem((8, 128), jnp.int32),
            pltpu.SMEM((8, 128), jnp.int32),
            vmem((MODES, 128, 128), F32),
            vmem((MODES, 32, 128), F32),
            vmem((MODES, 32, 128), F32),
            vmem((MODES, 32, 128), F32),
            pltpu.SemaphoreType.DMA((16,)),
            pltpu.SemaphoreType.DMA((N_SEND,)),
            pltpu.SemaphoreType.DMA((N_RECV,)),
        ],
        compiler_params=pltpu.CompilerParams(collective_id=0, has_side_effects=True),
    )(
        state,
        prev_slope,
        accumulated,
        hamiltonian,
        couple_v,
        coupling,
        damping,
        occupation,
        jnp.asarray(key_table()),
    )


def solution(mesh):
    block = P("hier", None, "row", None)
    return jax.shard_map(
        shards,
        mesh=mesh,
        in_specs=(
            block,
            block,
            block,
            P(None, "row", None),
            P(),
            P(),
            P(),
            P("hier", None),
            P("hier", None),
            P("hier", None),
        ),
        out_specs=(block, block),
        check_vma=False,
    )
```

```python
import jax
import jax.numpy as jnp
import numpy as np
from jax import lax
from jax.experimental import pallas as pl
from jax.experimental.pallas import tpu as pltpu
from jax.sharding import PartitionSpec as P

MESH = pl.DeviceIdType.MESH
N = 1024
MODES = 6
ADOS = 48
STEP = 0.5
F32 = jnp.float32
BF16 = jnp.bfloat16


def window_table():
    entries = [()]
    for _ in range(MODES):
        entries = [entry + (level,) for entry in entries for level in range(5)]
    chosen = [entry for entry in entries if sum(entry) <= 4]
    return sorted(chosen, key=lambda entry: (sum(entry), entry))[:ADOS]


TABLE = window_table()
PLACE = {entry: place for place, entry in enumerate(TABLE)}


def key_of(entry):
    return sum(entry[k] * 5**k for k in range(MODES))


def shifted(entry, mode, by):
    return PLACE.get(entry[:mode] + (entry[mode] + by,) + entry[mode + 1 :])


def key_table():
    keys = np.full((8, 128), -1, np.int32)
    keys[:, :ADOS] = [key_of(entry) for entry in TABLE]
    return keys


R_HN = 0
R_HU = 1
R_HD = 3
R_H2 = 5
R_HP = 9
R_L = 17
R_LP = 25
R_LR = 33
R_M = 41
R_A = 57
R_C = 89
N_RECV = 121
N_SEND = 140


def kernel(
    state,
    prev,
    acc,
    ham,
    cv_in,
    coup_in,
    damp_in,
    occ_in,
    tab_in,
    slope,
    acc_out,
    st_v,
    pv_v,
    acc_v,
    cv,
    tab,
    coup,
    damp,
    occ,
    sblk,
    amat,
    hv,
    mb,
    hn,
    lb,
    lout,
    lret,
    zin_0,
    zin_1,
    ccan,
    cout,
    cret,
    rbuf,
    slope_v,
    meta_out,
    meta_in,
    meta_v,
    meta_s,
    vt,
    dk,
    dg,
    eg,
    lsem,
    ssem,
    rsem,
):
    h = lax.axis_index("hier")
    r = lax.axis_index("row")
    xh, z = lax.div(h, 8), lax.rem(h, 8)
    p, c = lax.div(r, 2), lax.rem(r, 2)
    xl, y = lax.div(p, 4), lax.rem(p, 4)
    oc = 1 - c
    zin = (zin_0, zin_1)

    def chip(dx, dy):
        return lax.rem(xl + dx, 2) * 4 + lax.rem(y + dy, 4)

    def rowdev(dx, dy):
        return (h, chip(dx, dy) * 2 + c)

    def hier(dx, dz):
        return lax.rem(xh + dx, 2), lax.rem(z + dz, 8)

    other_core = (h, p * 2 + oc)
    x_cross = ((1 - xh) * 8 + z, ((1 - xl) * 4 + y) * 2 + c)

    row_offsets = [(dx, dy) for dy in (2, 1, 3, 0) for dx in (1, 0) if dx or dy]
    hier_offsets = [(dx, dz) for dz in (4, 3, 5, 2, 6, 1, 7, 0) for dx in (1, 0) if dx or dz]

    cp_h = pltpu.make_async_copy(ham, hv, lsem.at[0])
    cp_s = pltpu.make_async_copy(state, st_v, lsem.at[1])
    cp_p = pltpu.make_async_copy(prev, pv_v, lsem.at[2])
    cp_s.start()
    cp_p.start()
    cp_h.start()
    small = []
    for i, (src, dst) in enumerate(
        [(occ_in, occ), (tab_in, tab), (cv_in, cv), (coup_in, coup), (damp_in, damp), (acc, acc_v)]
    ):
        small.append(pltpu.make_async_copy(src, dst, lsem.at[10 + i]))
        small[i].start()

    barrier = pltpu.get_barrier_semaphore()
    greeted = []
    for dx, dz in hier_offsets:
        hx, hz = hier(dx, dz)
        greeted.append((hx * 8 + hz, r))
    greeted += [rowdev(dx, dy) for dx, dy in row_offsets]
    greeted += [x_cross, other_core]
    for dev in greeted:
        pl.semaphore_signal(barrier, inc=1, device_id=dev, device_id_type=MESH)

    for copy in small[:2]:
        copy.wait()
    lane = lax.broadcasted_iota(jnp.int32, (8, 128), 1)
    line = lax.broadcasted_iota(jnp.int32, (8, 128), 0)
    slots = jnp.zeros((8, 128), jnp.int32)
    places = jnp.zeros((8, 128), jnp.int32)
    for j in range(3):
        key = occ[j, 0]
        for k in range(1, MODES):
            key = key + occ[j, k] * (5**k)
        hit = tab[...] == key
        slots = slots + jnp.where(hit, 3 * h + j, 0)
        place = jnp.sum(jnp.where(hit, lane, 0), axis=1, keepdims=True)
        places = places + jnp.where(lane == 3 * h + j, place, 0)
    mine = jnp.where(line == 0, slots, places)
    meta_out[...] = mine
    meta_in[h] = mine

    cp_s.wait()
    cp_p.wait()

    @pl.loop(0, 3)
    def _(a):
        for quarter in range(4):
            rows = pl.ds(16 * quarter, 16)
            for b in range(8):
                cols = pl.ds(128 * b, 128)
                parts = []
                for ri in range(2):
                    value = st_v[a, ri, rows, cols].astype(F32) + (0.5 * STEP) * pv_v[a, ri, rows, cols]
                    parts.append(value.astype(BF16))
                    sblk[b, quarter, a, ri] = parts[ri]
                    amat[quarter, a, ri, :, cols] = parts[ri]
                late = pl.ds(N + 128 * b, 128)
                amat[quarter, a, 0, :, late] = -parts[1]
                amat[quarter, a, 1, :, late] = parts[0]

    cp_h.wait()
    across = lax.broadcasted_iota(jnp.int32, (64, N), 1)
    down = lax.broadcasted_iota(jnp.int32, (64, N), 0) + 64 * r
    mb[p, c] = jnp.where(across >= down, hv[0].astype(F32), hv[1].astype(F32)).astype(BF16)

    pl.semaphore_wait(barrier, len(greeted))

    sent = []

    def send(src, dst, to, dev):
        copy = pltpu.make_async_remote_copy(
            src_ref=src,
            dst_ref=dst,
            send_sem=ssem.at[len(sent)],
            recv_sem=rsem.at[to],
            device_id=dev,
            device_id_type=MESH,
        )
        copy.start()
        sent.append(copy)

    def arrived(dst, to):
        pltpu.make_async_remote_copy(
            src_ref=dst,
            dst_ref=dst,
            send_sem=ssem.at[0],
            recv_sem=rsem.at[to],
            device_id=other_core,
            device_id_type=MESH,
        ).wait_recv()

    def hblk(q):
        return mb.at[q, c]

    def send_h(q, to, dev):
        send(hblk(q), hblk(q), to, dev)

    def send_section(q):
        for dx, dz in hier_offsets:
            hx, hz = hier(dx, dz)
            dev = (hx * 8 + hz, r)
            if q == 0:
                send(meta_out, meta_in.at[h], R_M + 8 * dx + dz, dev)
            send(sblk.at[hz, 2 * hx + q], zin[q].at[pl.ds(3 * h, 3)], R_A + 16 * q + 8 * dx + dz, dev)

    def send_columns(way):
        for dx, dy in row_offsets:
            if dx == way:
                q = chip(dx, dy)
                send(sblk.at[q], lb.at[p, c], R_L + 4 * dx + dy, (h, q * 2 + c))

    send_h(p, R_HN, x_cross)
    send_h(p, R_HU, rowdev(0, 1))
    send_h(p, R_HD, rowdev(0, 3))
    send_section(0)
    send_h(p, R_HP, other_core)

    q = chip(1, 0)
    arrived(hblk(q), R_HN)
    send_h(q, R_HU + 1, rowdev(0, 1))
    send_h(q, R_HD + 1, rowdev(0, 3))
    send_columns(1)
    send_section(1)
    send_h(q, R_HP + 4, other_core)
    send(sblk.at[p], lb.at[p, c], R_LP, other_core)
    lb[p, c] = sblk[p]
    for q in range(2):
        zin[q][pl.ds(3 * h, 3)] = sblk[z, 2 * xh + q]

    for copy in small[2:]:
        copy.wait()
    for k in range(MODES):
        line_v = cv[pl.ds(k, 1), pl.ds(pl.multiple_of(128 * p, 128), 128)]
        vt[k] = jnp.broadcast_to(line_v, (128, 128)).T
        v_rows = vt[k, pl.ds(pl.multiple_of(64 * c + 32 * xh, 32), 32), :]
        v_cols = cv[pl.ds(k, 1), pl.ds(pl.multiple_of(128 * z, 128), 128)]
        diff = v_rows - v_cols
        dk[k] = diff
        dg[k] = coup[0, k] * diff
        eg[k] = coup[1, k] * (v_rows + v_cols)

    def half_h(q, half):
        return mb.at[q, c, pl.ds(32 * half, 32)]

    for dx in range(2):
        below, above = chip(dx, 3), chip(dx, 1)
        arrived(hblk(below), R_HU + dx)
        send(half_h(below, 0), half_h(below, 0), R_H2 + 2 * dx, rowdev(0, 1))
        arrived(hblk(above), R_HD + dx)
        send(half_h(above, 1), half_h(above, 1), R_H2 + 2 * dx + 1, rowdev(0, 3))
        send_h(below, R_HP + 4 * dx + 3, other_core)
        send_h(above, R_HP + 4 * dx + 1, other_core)
    send_columns(0)
    for dx in range(2):
        q = chip(dx, 2)
        arrived(half_h(q, 0), R_H2 + 2 * dx)
        arrived(half_h(q, 1), R_H2 + 2 * dx + 1)
        send_h(q, R_HP + 4 * dx + 2, other_core)

    for dx, dz in hier_offsets:
        hx, hz = hier(dx, 8 - dz)
        arrived(meta_in.at[hx * 8 + hz], R_M + 8 * dx + dz)
    meta_v[...] = jnp.minimum(jnp.sum(meta_in[...], axis=0), ADOS - 1)
    cp_m = pltpu.make_async_copy(meta_v, meta_s, lsem.at[3])
    cp_m.start()
    cp_m.wait()

    def couple(q):
        for dx, dz in hier_offsets:
            hx, hz = hier(dx, 8 - dz)
            arrived(zin[q].at[pl.ds(3 * (hx * 8 + hz), 3)], R_A + 16 * q + 8 * dx + dz)
        rows = pl.ds(16 * q, 16)
        for place, entry in enumerate(TABLE):
            re = jnp.zeros((16, 128), F32)
            im = jnp.zeros((16, 128), F32)
            for k in range(MODES):
                child = shifted(entry, k, 1)
                if child is not None:
                    near = zin[q][meta_s[0, child]].astype(F32)
                    re = re + dk[k, rows] * near[1]
                    im = im - dk[k, rows] * near[0]
                if entry[k] > 0:
                    near = zin[q][meta_s[0, shifted(entry, k, -1)]].astype(F32)
                    add_re = dg[k, rows] * near[1] + eg[k, rows] * near[0]
                    add_im = eg[k, rows] * near[1] - dg[k, rows] * near[0]
                    if entry[k] > 1:
                        add_re = add_re * float(entry[k])
                        add_im = add_im * float(entry[k])
                    re = re + add_re
                    im = im + add_im
            ccan[place, 0] = re.astype(BF16)
            ccan[place, 1] = im.astype(BF16)
        for slot in range(ADOS):
            cout[q, slot] = ccan[meta_s[1, slot]]
        for dx, dz in hier_offsets:
            hx, hz = hier(dx, dz)
            to = hx * 8 + hz
            send(cout.at[q, pl.ds(3 * to, 3)], cret.at[2 * xh + q, z], R_C + 16 * q + 8 * dx + dz, (to, r))
        cret[2 * xh + q, z] = cout[q, pl.ds(3 * h, 3)]

    couple(0)

    for dx in range(2):
        for dy in range(4):
            arrived(mb.at[chip(dx, dy), oc], R_HP + 4 * dx + dy)
    under = lax.broadcasted_iota(jnp.int32, (128, 128), 0)
    along = lax.broadcasted_iota(jnp.int32, (128, 128), 1)

    def put(ri, i, j, tile):
        hn[ri, i, :, :, pl.ds(128 * j, 128)] = tile.reshape(2, 64, 128)

    for i in range(8):
        for j in range(i, 8):
            upper = mb[i, :, :, pl.ds(128 * j, 128)].reshape(128, 128)
            if i == j:
                wide = upper.astype(F32)
                flipped = wide.T
                put(0, i, i, jnp.where(along >= under, wide, flipped).astype(BF16))
                below = jnp.where(along > under, -flipped, 0.0)
                put(1, i, i, jnp.where(along < under, wide, below).astype(BF16))
            else:
                lower = mb[j, :, :, pl.ds(128 * i, 128)].reshape(128, 128)
                put(0, i, j, upper)
                put(0, j, i, upper.T)
                put(1, i, j, -lower.T)
                put(1, j, i, lower)

    for dx, dy in row_offsets:
        back = (4 - dy) % 4
        q = chip(dx, back)
        arrived(lb.at[q, c], R_L + 4 * dx + dy)
        send(lb.at[q, c], lb.at[q, c], R_LP + 4 * dx + back, other_core)

    couple(1)

    for dx in range(2):
        for dy in range(4):
            arrived(lb.at[chip(dx, dy), oc], R_LP + 4 * dx + dy)

    @pl.loop(0, 3)
    def _(a):
        real = lb[:, :, :, a, 0].reshape(N, 128)
        imag = lb[:, :, :, a, 1].reshape(N, 128)
        rhs = jnp.concatenate(
            [jnp.concatenate([real, imag], 1), jnp.concatenate([-imag, real], 1)], 0
        )
        for m in range(2):
            lhs = jnp.concatenate(
                [hn[ri, pl.ds(4 * m, 4), c].reshape(256, N) for ri in range(2)], 1
            )
            out = jnp.dot(lhs, rhs, preferred_element_type=F32).astype(BF16)
            out = out.reshape(4, 4, 16, 256)
            lout[pl.ds(4 * m, 4), :, a, 0] = out[..., :128]
            lout[pl.ds(4 * m, 4), :, a, 1] = out[..., 128:]

    for dx, dy in row_offsets:
        q = chip(dx, dy)
        send(lout.at[q], lret.at[p], R_LR + 4 * dx + dy, (h, q * 2 + c))
    lret[p] = lout[p]

    @pl.loop(0, 4)
    def _(n):
        cols = pl.ds(pl.multiple_of(256 * n, 256), 256)
        rhs = jnp.concatenate(
            [hn[ri, :, :, :, cols].reshape(N, 256) for ri in range(2)], 0
        )
        lhs = amat[...].reshape(384, 2 * N)
        out = jnp.dot(lhs, rhs, preferred_element_type=F32)
        rbuf[:, :, :, :, cols] = out.reshape(4, 3, 2, 16, 256)

    for q in range(2):
        for dx, dz in hier_offsets:
            hx, hz = hier(dx, 8 - dz)
            arrived(cret.at[2 * hx + q, hz], R_C + 16 * q + 8 * dx + dz)
    for dx, dy in row_offsets:
        back = (4 - dy) % 4
        arrived(lret.at[chip(dx, back)], R_LR + 4 * dx + dy)

    @pl.loop(0, 3)
    def _(a):
        decay = occ[a, 0].astype(F32) * damp[0]
        for k in range(1, MODES):
            decay = decay + occ[a, k].astype(F32) * damp[k]
        for quarter in range(4):
            for b in range(8):
                cols = pl.ds(128 * b, 128)
                for ri in range(2):
                    turned = lret[b, quarter, a, 1 - ri].astype(F32) - rbuf[quarter, a, 1 - ri, :, cols]
                    if ri:
                        turned = -turned
                    value = turned - decay * sblk[b, quarter, a, ri].astype(F32)
                    value = value + cret[quarter, b, a, ri].astype(F32)
                    rows = pl.ds(16 * quarter, 16)
                    slope_v[a, ri, rows, cols] = value
                    pv_v[a, ri, rows, cols] = acc_v[a, ri, rows, cols] + (STEP / 3.0) * value
        pltpu.make_async_copy(slope_v.at[a], slope.at[a], lsem.at[4 + a]).start()
        pltpu.make_async_copy(pv_v.at[a], acc_out.at[a], lsem.at[7 + a]).start()

    for a in range(3):
        pltpu.make_async_copy(slope_v.at[a], slope.at[a], lsem.at[4 + a]).wait()
        pltpu.make_async_copy(pv_v.at[a], acc_out.at[a], lsem.at[7 + a]).wait()
    for copy in sent:
        copy.wait_send()


def shards(state, prev_slope, accumulated, hamiltonian, couple_v, coupling, damping, occupation, parents, children):
    vmem = pltpu.VMEM
    anywhere = pl.BlockSpec(memory_space=pl.ANY)
    block = jax.ShapeDtypeStruct((3, 2, 64, N), F32)
    return pl.pallas_call(
        kernel,
        name="section",
        out_shape=(block, block),
        in_specs=[anywhere] * 9,
        out_specs=(anywhere, anywhere),
        scratch_shapes=[
            vmem((3, 2, 64, N), BF16),
            vmem((3, 2, 64, N), F32),
            vmem((3, 2, 64, N), F32),
            vmem((MODES, N), F32),
            vmem((8, 128), jnp.int32),
            pltpu.SMEM((2, MODES), F32),
            pltpu.SMEM((MODES,), F32),
            pltpu.SMEM((3, MODES), jnp.int32),
            vmem((8, 4, 3, 2, 16, 128), BF16),
            vmem((4, 3, 2, 16, 2 * N), BF16),
            vmem((2, 64, N), BF16),
            vmem((8, 2, 64, N), BF16),
            vmem((2, 8, 2, 64, N), BF16),
            vmem((8, 2, 4, 3, 2, 16, 128), BF16),
            vmem((8, 4, 3, 2, 16, 128), BF16),
            vmem((8, 4, 3, 2, 16, 128), BF16),
            vmem((ADOS, 2, 16, 128), BF16),
            vmem((ADOS, 2, 16, 128), BF16),
            vmem((ADOS, 2, 16, 128), BF16),
            vmem((2, ADOS, 2, 16, 128), BF16),
            vmem((4, 8, 3, 2, 16, 128), BF16),
            vmem((4, 3, 2, 16, N), F32),
            vmem((3, 2, 64, N), F32),
            vmem((8, 128), jnp.int32),
            vmem((16, 8, 128), jnp.int32),
            vmem((8, 128), jnp.int32),
            pltpu.SMEM((8, 128), jnp.int32),
            vmem((MODES, 128, 128), F32),
            vmem((MODES, 32, 128), F32),
            vmem((MODES, 32, 128), F32),
            vmem((MODES, 32, 128), F32),
            pltpu.SemaphoreType.DMA((16,)),
            pltpu.SemaphoreType.DMA((N_SEND,)),
            pltpu.SemaphoreType.DMA((N_RECV,)),
        ],
        compiler_params=pltpu.CompilerParams(collective_id=0, has_side_effects=True),
    )(
        state,
        prev_slope,
        accumulated,
        hamiltonian,
        couple_v,
        coupling,
        damping,
        occupation,
        jnp.asarray(key_table()),
    )


def solution(mesh):
    block = P("hier", None, "row", None)
    return jax.shard_map(
        shards,
        mesh=mesh,
        in_specs=(
            block,
            block,
            block,
            P(None, "row", None),
            P(),
            P(),
            P(),
            P("hier", None),
            P("hier", None),
            P("hier", None),
        ),
        out_specs=(block, block),
        check_vma=False,
    )
```

```python
import jax
import jax.numpy as jnp
import numpy as np
from jax import lax
from jax.experimental import pallas as pl
from jax.experimental.pallas import tpu as pltpu
from jax.sharding import PartitionSpec as P

MESH = pl.DeviceIdType.MESH
N = 1024
MODES = 6
ADOS = 48
STEP = 0.5
F32 = jnp.float32
BF16 = jnp.bfloat16


def window_table():
    entries = [()]
    for _ in range(MODES):
        entries = [entry + (level,) for entry in entries for level in range(5)]
    chosen = [entry for entry in entries if sum(entry) <= 4]
    return sorted(chosen, key=lambda entry: (sum(entry), entry))[:ADOS]


TABLE = window_table()
PLACE = {entry: place for place, entry in enumerate(TABLE)}


def key_of(entry):
    return sum(entry[k] * 5**k for k in range(MODES))


def shifted(entry, mode, by):
    return PLACE.get(entry[:mode] + (entry[mode] + by,) + entry[mode + 1 :])


def key_table():
    keys = np.full((8, 128), -1, np.int32)
    keys[:, :ADOS] = [key_of(entry) for entry in TABLE]
    return keys


R_HN = 0
R_HU = 1
R_HD = 3
R_H2 = 5
R_HP = 9
R_L = 17
R_LP = 25
R_LR = 33
R_M = 41
R_A = 57
R_C = 89
N_RECV = 121
N_SEND = 140


def kernel(
    state,
    prev,
    acc,
    ham,
    cv_in,
    coup_in,
    damp_in,
    occ_in,
    tab_in,
    slope,
    acc_out,
    st_v,
    pv_v,
    acc_v,
    cv,
    tab,
    coup,
    damp,
    occ,
    sblk,
    amat,
    hv,
    mb,
    hn,
    lb,
    lout,
    lret,
    zin_0,
    zin_1,
    ccan,
    cout,
    cret,
    rbuf,
    meta_out,
    meta_in,
    meta_v,
    meta_s,
    vt,
    dk,
    dg,
    eg,
    lsem,
    ssem,
    rsem,
):
    h = lax.axis_index("hier")
    r = lax.axis_index("row")
    xh, z = lax.div(h, 8), lax.rem(h, 8)
    p, c = lax.div(r, 2), lax.rem(r, 2)
    xl, y = lax.div(p, 4), lax.rem(p, 4)
    oc = 1 - c
    zin = (zin_0, zin_1)

    def chip(dx, dy):
        return lax.rem(xl + dx, 2) * 4 + lax.rem(y + dy, 4)

    def rowdev(dx, dy):
        return (h, chip(dx, dy) * 2 + c)

    def hier(dx, dz):
        return lax.rem(xh + dx, 2), lax.rem(z + dz, 8)

    other_core = (h, p * 2 + oc)
    x_cross = ((1 - xh) * 8 + z, ((1 - xl) * 4 + y) * 2 + c)

    row_offsets = [(dx, dy) for dy in (2, 1, 3, 0) for dx in (1, 0) if dx or dy]
    hier_offsets = [(dx, dz) for dz in (4, 3, 5, 2, 6, 1, 7, 0) for dx in (1, 0) if dx or dz]

    cp_h = pltpu.make_async_copy(ham, hv, lsem.at[0])
    cp_s = pltpu.make_async_copy(state, st_v, lsem.at[1])
    cp_p = pltpu.make_async_copy(prev, pv_v, lsem.at[2])
    cp_s.start()
    cp_p.start()
    cp_h.start()
    small = []
    for i, (src, dst) in enumerate(
        [(occ_in, occ), (tab_in, tab), (cv_in, cv), (coup_in, coup), (damp_in, damp), (acc, acc_v)]
    ):
        small.append(pltpu.make_async_copy(src, dst, lsem.at[10 + i]))
        small[i].start()

    barrier = pltpu.get_barrier_semaphore()
    greeted = []
    for dx, dz in hier_offsets:
        hx, hz = hier(dx, dz)
        greeted.append((hx * 8 + hz, r))
    greeted += [rowdev(dx, dy) for dx, dy in row_offsets]
    greeted += [x_cross, other_core]
    for dev in greeted:
        pl.semaphore_signal(barrier, inc=1, device_id=dev, device_id_type=MESH)

    for copy in small[:2]:
        copy.wait()
    lane = lax.broadcasted_iota(jnp.int32, (8, 128), 1)
    line = lax.broadcasted_iota(jnp.int32, (8, 128), 0)
    slots = jnp.zeros((8, 128), jnp.int32)
    places = jnp.zeros((8, 128), jnp.int32)
    for j in range(3):
        key = occ[j, 0]
        for k in range(1, MODES):
            key = key + occ[j, k] * (5**k)
        hit = tab[...] == key
        slots = slots + jnp.where(hit, 3 * h + j, 0)
        place = jnp.sum(jnp.where(hit, lane, 0), axis=1, keepdims=True)
        places = places + jnp.where(lane == 3 * h + j, place, 0)
    mine = jnp.where(line == 0, slots, places)
    meta_out[...] = mine
    meta_in[h] = mine

    cp_s.wait()
    cp_p.wait()

    @pl.loop(0, 3)
    def _(a):
        for quarter in range(4):
            rows = pl.ds(16 * quarter, 16)
            for b in range(8):
                cols = pl.ds(128 * b, 128)
                parts = []
                for ri in range(2):
                    value = st_v[a, ri, rows, cols].astype(F32) + (0.5 * STEP) * pv_v[a, ri, rows, cols]
                    parts.append(value.astype(BF16))
                    sblk[b, quarter, a, ri] = parts[ri]
                    amat[quarter, a, ri, :, cols] = parts[ri]
                late = pl.ds(N + 128 * b, 128)
                amat[quarter, a, 0, :, late] = -parts[1]
                amat[quarter, a, 1, :, late] = parts[0]

    cp_h.wait()
    across = lax.broadcasted_iota(jnp.int32, (64, N), 1)
    down = lax.broadcasted_iota(jnp.int32, (64, N), 0) + 64 * r
    mb[p, c] = jnp.where(across >= down, hv[0].astype(F32), hv[1].astype(F32)).astype(BF16)

    pl.semaphore_wait(barrier, len(greeted))

    sent = []

    def send(src, dst, to, dev):
        copy = pltpu.make_async_remote_copy(
            src_ref=src,
            dst_ref=dst,
            send_sem=ssem.at[len(sent)],
            recv_sem=rsem.at[to],
            device_id=dev,
            device_id_type=MESH,
        )
        copy.start()
        sent.append(copy)

    def arrived(dst, to):
        pltpu.make_async_remote_copy(
            src_ref=dst,
            dst_ref=dst,
            send_sem=ssem.at[0],
            recv_sem=rsem.at[to],
            device_id=other_core,
            device_id_type=MESH,
        ).wait_recv()

    def hblk(q):
        return mb.at[q, c]

    def send_h(q, to, dev):
        send(hblk(q), hblk(q), to, dev)

    def send_section(q):
        for dx, dz in hier_offsets:
            hx, hz = hier(dx, dz)
            dev = (hx * 8 + hz, r)
            if q == 0:
                send(meta_out, meta_in.at[h], R_M + 8 * dx + dz, dev)
            send(sblk.at[hz, 2 * hx + q], zin[q].at[pl.ds(3 * h, 3)], R_A + 16 * q + 8 * dx + dz, dev)

    def send_columns(way):
        for dx, dy in row_offsets:
            if dx == way:
                q = chip(dx, dy)
                send(sblk.at[q], lb.at[p, c], R_L + 4 * dx + dy, (h, q * 2 + c))

    send_h(p, R_HN, x_cross)
    send_h(p, R_HU, rowdev(0, 1))
    send_h(p, R_HD, rowdev(0, 3))
    send_section(0)
    send_h(p, R_HP, other_core)

    q = chip(1, 0)
    arrived(hblk(q), R_HN)
    send_h(q, R_HU + 1, rowdev(0, 1))
    send_h(q, R_HD + 1, rowdev(0, 3))
    send_columns(1)
    send_section(1)
    send_h(q, R_HP + 4, other_core)
    send(sblk.at[p], lb.at[p, c], R_LP, other_core)
    lb[p, c] = sblk[p]
    for q in range(2):
        zin[q][pl.ds(3 * h, 3)] = sblk[z, 2 * xh + q]

    for copy in small[2:]:
        copy.wait()
    for k in range(MODES):
        line_v = cv[pl.ds(k, 1), pl.ds(pl.multiple_of(128 * p, 128), 128)]
        vt[k] = jnp.broadcast_to(line_v, (128, 128)).T
        v_rows = vt[k, pl.ds(pl.multiple_of(64 * c + 32 * xh, 32), 32), :]
        v_cols = cv[pl.ds(k, 1), pl.ds(pl.multiple_of(128 * z, 128), 128)]
        diff = v_rows - v_cols
        dk[k] = diff
        dg[k] = coup[0, k] * diff
        eg[k] = coup[1, k] * (v_rows + v_cols)

    def half_h(q, half):
        return mb.at[q, c, pl.ds(32 * half, 32)]

    for dx in range(2):
        below, above = chip(dx, 3), chip(dx, 1)
        arrived(hblk(below), R_HU + dx)
        send(half_h(below, 0), half_h(below, 0), R_H2 + 2 * dx, rowdev(0, 1))
        arrived(hblk(above), R_HD + dx)
        send(half_h(above, 1), half_h(above, 1), R_H2 + 2 * dx + 1, rowdev(0, 3))
        send_h(below, R_HP + 4 * dx + 3, other_core)
        send_h(above, R_HP + 4 * dx + 1, other_core)
    send_columns(0)
    for dx in range(2):
        q = chip(dx, 2)
        arrived(half_h(q, 0), R_H2 + 2 * dx)
        arrived(half_h(q, 1), R_H2 + 2 * dx + 1)
        send_h(q, R_HP + 4 * dx + 2, other_core)

    for dx, dz in hier_offsets:
        hx, hz = hier(dx, 8 - dz)
        arrived(meta_in.at[hx * 8 + hz], R_M + 8 * dx + dz)
    meta_v[...] = jnp.minimum(jnp.sum(meta_in[...], axis=0), ADOS - 1)
    cp_m = pltpu.make_async_copy(meta_v, meta_s, lsem.at[3])
    cp_m.start()
    cp_m.wait()

    def couple(q):
        for dx, dz in hier_offsets:
            hx, hz = hier(dx, 8 - dz)
            arrived(zin[q].at[pl.ds(3 * (hx * 8 + hz), 3)], R_A + 16 * q + 8 * dx + dz)
        rows = pl.ds(16 * q, 16)
        for place, entry in enumerate(TABLE):
            re = jnp.zeros((16, 128), F32)
            im = jnp.zeros((16, 128), F32)
            for k in range(MODES):
                child = shifted(entry, k, 1)
                if child is not None:
                    near = zin[q][meta_s[0, child]].astype(F32)
                    re = re + dk[k, rows] * near[1]
                    im = im - dk[k, rows] * near[0]
                if entry[k] > 0:
                    near = zin[q][meta_s[0, shifted(entry, k, -1)]].astype(F32)
                    add_re = dg[k, rows] * near[1] + eg[k, rows] * near[0]
                    add_im = eg[k, rows] * near[1] - dg[k, rows] * near[0]
                    if entry[k] > 1:
                        add_re = add_re * float(entry[k])
                        add_im = add_im * float(entry[k])
                    re = re + add_re
                    im = im + add_im
            ccan[place, 0] = re.astype(BF16)
            ccan[place, 1] = im.astype(BF16)
        for slot in range(ADOS):
            cout[q, slot] = ccan[meta_s[1, slot]]
        for dx, dz in hier_offsets:
            hx, hz = hier(dx, dz)
            to = hx * 8 + hz
            send(cout.at[q, pl.ds(3 * to, 3)], cret.at[2 * xh + q, z], R_C + 16 * q + 8 * dx + dz, (to, r))
        cret[2 * xh + q, z] = cout[q, pl.ds(3 * h, 3)]

    couple(0)

    for dx in range(2):
        for dy in range(4):
            arrived(mb.at[chip(dx, dy), oc], R_HP + 4 * dx + dy)
    under = lax.broadcasted_iota(jnp.int32, (128, 128), 0)
    along = lax.broadcasted_iota(jnp.int32, (128, 128), 1)

    def put(ri, i, j, tile):
        hn[ri, i, :, :, pl.ds(128 * j, 128)] = tile.reshape(2, 64, 128)

    for i in range(8):
        for j in range(i, 8):
            upper = mb[i, :, :, pl.ds(128 * j, 128)].reshape(128, 128)
            if i == j:
                wide = upper.astype(F32)
                flipped = wide.T
                put(0, i, i, jnp.where(along >= under, wide, flipped).astype(BF16))
                below = jnp.where(along > under, -flipped, 0.0)
                put(1, i, i, jnp.where(along < under, wide, below).astype(BF16))
            else:
                lower = mb[j, :, :, pl.ds(128 * i, 128)].reshape(128, 128)
                put(0, i, j, upper)
                put(0, j, i, upper.T)
                put(1, i, j, -lower.T)
                put(1, j, i, lower)

    for dx, dy in row_offsets:
        back = (4 - dy) % 4
        q = chip(dx, back)
        arrived(lb.at[q, c], R_L + 4 * dx + dy)
        send(lb.at[q, c], lb.at[q, c], R_LP + 4 * dx + back, other_core)

    couple(1)

    for dx in range(2):
        for dy in range(4):
            arrived(lb.at[chip(dx, dy), oc], R_LP + 4 * dx + dy)

    @pl.loop(0, 3)
    def _(a):
        real = lb[:, :, :, a, 0].reshape(N, 128)
        imag = lb[:, :, :, a, 1].reshape(N, 128)
        rhs = jnp.concatenate(
            [jnp.concatenate([real, imag], 1), jnp.concatenate([-imag, real], 1)], 0
        )
        for m in range(2):
            lhs = jnp.concatenate(
                [hn[ri, pl.ds(4 * m, 4), c].reshape(256, N) for ri in range(2)], 1
            )
            out = jnp.dot(lhs, rhs, preferred_element_type=F32).astype(BF16)
            out = out.reshape(4, 4, 16, 256)
            lout[pl.ds(4 * m, 4), :, a, 0] = out[..., :128]
            lout[pl.ds(4 * m, 4), :, a, 1] = out[..., 128:]

    for dx, dy in row_offsets:
        q = chip(dx, dy)
        send(lout.at[q], lret.at[p], R_LR + 4 * dx + dy, (h, q * 2 + c))
    lret[p] = lout[p]

    @pl.loop(0, 4)
    def _(n):
        cols = pl.ds(pl.multiple_of(256 * n, 256), 256)
        rhs = jnp.concatenate(
            [hn[ri, :, :, :, cols].reshape(N, 256) for ri in range(2)], 0
        )
        lhs = amat[...].reshape(384, 2 * N)
        out = jnp.dot(lhs, rhs, preferred_element_type=F32)
        rbuf[:, :, :, :, cols] = out.reshape(4, 3, 2, 16, 256)

    for q in range(2):
        for dx, dz in hier_offsets:
            hx, hz = hier(dx, 8 - dz)
            arrived(cret.at[2 * hx + q, hz], R_C + 16 * q + 8 * dx + dz)
    for dx, dy in row_offsets:
        back = (4 - dy) % 4
        arrived(lret.at[chip(dx, back)], R_LR + 4 * dx + dy)

    @pl.loop(0, 3)
    def _(a):
        decay = occ[a, 0].astype(F32) * damp[0]
        for k in range(1, MODES):
            decay = decay + occ[a, k].astype(F32) * damp[k]
        for quarter in range(4):
            for b in range(8):
                cols = pl.ds(128 * b, 128)
                for ri in range(2):
                    turned = lret[b, quarter, a, 1 - ri].astype(F32) - rbuf[quarter, a, 1 - ri, :, cols]
                    if ri:
                        turned = -turned
                    value = turned - decay * sblk[b, quarter, a, ri].astype(F32)
                    value = value + cret[quarter, b, a, ri].astype(F32)
                    rows = pl.ds(16 * quarter, 16)
                    slope[a, ri, rows, cols] = value
                    acc_out[a, ri, rows, cols] = acc_v[a, ri, rows, cols] + (STEP / 3.0) * value

    for copy in sent:
        copy.wait_send()


def shards(state, prev_slope, accumulated, hamiltonian, couple_v, coupling, damping, occupation, parents, children):
    vmem = pltpu.VMEM
    anywhere = pl.BlockSpec(memory_space=pl.ANY)
    in_vmem = pl.BlockSpec(memory_space=pltpu.VMEM)
    block = vmem((3, 2, 64, N), F32)
    return pl.pallas_call(
        kernel,
        name="section",
        out_shape=(block, block),
        in_specs=[anywhere] * 9,
        out_specs=(in_vmem, in_vmem),
        scratch_shapes=[
            vmem((3, 2, 64, N), BF16),
            vmem((3, 2, 64, N), F32),
            vmem((3, 2, 64, N), F32),
            vmem((MODES, N), F32),
            vmem((8, 128), jnp.int32),
            pltpu.SMEM((2, MODES), F32),
            pltpu.SMEM((MODES,), F32),
            pltpu.SMEM((3, MODES), jnp.int32),
            vmem((8, 4, 3, 2, 16, 128), BF16),
            vmem((4, 3, 2, 16, 2 * N), BF16),
            vmem((2, 64, N), BF16),
            vmem((8, 2, 64, N), BF16),
            vmem((2, 8, 2, 64, N), BF16),
            vmem((8, 2, 4, 3, 2, 16, 128), BF16),
            vmem((8, 4, 3, 2, 16, 128), BF16),
            vmem((8, 4, 3, 2, 16, 128), BF16),
            vmem((ADOS, 2, 16, 128), BF16),
            vmem((ADOS, 2, 16, 128), BF16),
            vmem((ADOS, 2, 16, 128), BF16),
            vmem((2, ADOS, 2, 16, 128), BF16),
            vmem((4, 8, 3, 2, 16, 128), BF16),
            vmem((4, 3, 2, 16, N), F32),
            vmem((8, 128), jnp.int32),
            vmem((16, 8, 128), jnp.int32),
            vmem((8, 128), jnp.int32),
            pltpu.SMEM((8, 128), jnp.int32),
            vmem((MODES, 128, 128), F32),
            vmem((MODES, 32, 128), F32),
            vmem((MODES, 32, 128), F32),
            vmem((MODES, 32, 128), F32),
            pltpu.SemaphoreType.DMA((16,)),
            pltpu.SemaphoreType.DMA((N_SEND,)),
            pltpu.SemaphoreType.DMA((N_RECV,)),
        ],
        compiler_params=pltpu.CompilerParams(collective_id=0, has_side_effects=True),
    )(
        state,
        prev_slope,
        accumulated,
        hamiltonian,
        couple_v,
        coupling,
        damping,
        occupation,
        jnp.asarray(key_table()),
    )


def solution(mesh):
    block = P("hier", None, "row", None)
    return jax.shard_map(
        shards,
        mesh=mesh,
        in_specs=(
            block,
            block,
            block,
            P(None, "row", None),
            P(),
            P(),
            P(),
            P("hier", None),
            P("hier", None),
            P("hier", None),
        ),
        out_specs=(block, block),
        check_vma=False,
    )
```

```python
import jax
import jax.numpy as jnp
import numpy as np
from jax import lax
from jax.experimental import pallas as pl
from jax.experimental.pallas import tpu as pltpu
from jax.sharding import PartitionSpec as P

MESH = pl.DeviceIdType.MESH
N = 1024
MODES = 6
ADOS = 48
STEP = 0.5
F32 = jnp.float32
BF16 = jnp.bfloat16


def window_table():
    entries = [()]
    for _ in range(MODES):
        entries = [entry + (level,) for entry in entries for level in range(5)]
    chosen = [entry for entry in entries if sum(entry) <= 4]
    return sorted(chosen, key=lambda entry: (sum(entry), entry))[:ADOS]


TABLE = window_table()
PLACE = {entry: place for place, entry in enumerate(TABLE)}


def key_of(entry):
    return sum(entry[k] * 5**k for k in range(MODES))


def shifted(entry, mode, by):
    return PLACE.get(entry[:mode] + (entry[mode] + by,) + entry[mode + 1 :])


def key_table():
    keys = np.full((8, 128), -1, np.int32)
    keys[:, :ADOS] = [key_of(entry) for entry in TABLE]
    return keys


R_HN = 0
R_HU = 1
R_HD = 3
R_H2 = 5
R_HP = 9
R_L = 17
R_LP = 25
R_LR = 33
R_M = 41
R_A = 57
R_C = 89
N_RECV = 121
N_SEND = 140


def kernel(
    state,
    prev,
    acc,
    ham,
    cv_in,
    coup_in,
    damp_in,
    occ_in,
    tab_in,
    slope,
    acc_out,
    st_v,
    pv_v,
    acc_v,
    cv,
    tab,
    coup,
    damp,
    occ,
    sblk,
    amat,
    hv,
    mb,
    hn,
    lb,
    lout,
    lret,
    zin_0,
    zin_1,
    ccan,
    cout,
    cret,
    rbuf,
    meta_out,
    meta_in,
    meta_v,
    meta_s,
    vt,
    dk,
    dg,
    eg,
    lsem,
    ssem,
    rsem,
):
    h = lax.axis_index("hier")
    r = lax.axis_index("row")
    xh, z = lax.div(h, 8), lax.rem(h, 8)
    p, c = lax.div(r, 2), lax.rem(r, 2)
    xl, y = lax.div(p, 4), lax.rem(p, 4)
    oc = 1 - c
    zin = (zin_0, zin_1)

    def chip(dx, dy):
        return lax.rem(xl + dx, 2) * 4 + lax.rem(y + dy, 4)

    def rowdev(dx, dy):
        return (h, chip(dx, dy) * 2 + c)

    def hier(dx, dz):
        return lax.rem(xh + dx, 2), lax.rem(z + dz, 8)

    other_core = (h, p * 2 + oc)
    x_cross = ((1 - xh) * 8 + z, ((1 - xl) * 4 + y) * 2 + c)

    row_offsets = [(dx, dy) for dy in (2, 1, 3, 0) for dx in (1, 0) if dx or dy]
    hier_offsets = [(dx, dz) for dz in (4, 3, 5, 2, 6, 1, 7, 0) for dx in (1, 0) if dx or dz]

    cp_h = pltpu.make_async_copy(ham, hv, lsem.at[0])
    cp_s = pltpu.make_async_copy(state, st_v, lsem.at[1])
    cp_p = pltpu.make_async_copy(prev, pv_v, lsem.at[2])
    cp_s.start()
    cp_p.start()
    cp_h.start()
    small = []
    for i, (src, dst) in enumerate(
        [(occ_in, occ), (tab_in, tab), (cv_in, cv), (coup_in, coup), (damp_in, damp), (acc, acc_v)]
    ):
        small.append(pltpu.make_async_copy(src, dst, lsem.at[10 + i]))
        small[i].start()

    barrier = pltpu.get_barrier_semaphore()
    greeted = []
    for dx, dz in hier_offsets:
        hx, hz = hier(dx, dz)
        greeted.append((hx * 8 + hz, r))
    greeted += [rowdev(dx, dy) for dx, dy in row_offsets]
    greeted += [x_cross, other_core]
    for dev in greeted:
        pl.semaphore_signal(barrier, inc=1, device_id=dev, device_id_type=MESH)

    for copy in small[:2]:
        copy.wait()
    lane = lax.broadcasted_iota(jnp.int32, (8, 128), 1)
    line = lax.broadcasted_iota(jnp.int32, (8, 128), 0)
    slots = jnp.zeros((8, 128), jnp.int32)
    places = jnp.zeros((8, 128), jnp.int32)
    for j in range(3):
        key = occ[j, 0]
        for k in range(1, MODES):
            key = key + occ[j, k] * (5**k)
        hit = tab[...] == key
        slots = slots + jnp.where(hit, 3 * h + j, 0)
        place = jnp.sum(jnp.where(hit, lane, 0), axis=1, keepdims=True)
        places = places + jnp.where(lane == 3 * h + j, place, 0)
    mine = jnp.where(line == 0, slots, places)
    meta_out[...] = mine
    meta_in[h] = mine

    cp_s.wait()
    cp_p.wait()

    @pl.loop(0, 3)
    def _(a):
        for quarter in range(4):
            rows = pl.ds(16 * quarter, 16)
            for b in range(8):
                cols = pl.ds(128 * b, 128)
                parts = []
                for ri in range(2):
                    value = st_v[a, ri, rows, cols].astype(F32) + (0.5 * STEP) * pv_v[a, ri, rows, cols]
                    parts.append(value.astype(BF16))
                    sblk[b, quarter, a, ri] = parts[ri]
                    amat[quarter, a, ri, :, cols] = parts[ri]
                late = pl.ds(N + 128 * b, 128)
                amat[quarter, a, 0, :, late] = -parts[1]
                amat[quarter, a, 1, :, late] = parts[0]

    cp_h.wait()
    across = lax.broadcasted_iota(jnp.int32, (64, N), 1)
    down = lax.broadcasted_iota(jnp.int32, (64, N), 0) + 64 * r
    mb[p, c] = jnp.where(across >= down, hv[0].astype(F32), hv[1].astype(F32)).astype(BF16)

    pl.semaphore_wait(barrier, len(greeted))

    sent = []

    def send(src, dst, to, dev):
        copy = pltpu.make_async_remote_copy(
            src_ref=src,
            dst_ref=dst,
            send_sem=ssem.at[len(sent)],
            recv_sem=rsem.at[to],
            device_id=dev,
            device_id_type=MESH,
        )
        copy.start()
        sent.append(copy)

    def arrived(dst, to):
        pltpu.make_async_remote_copy(
            src_ref=dst,
            dst_ref=dst,
            send_sem=ssem.at[0],
            recv_sem=rsem.at[to],
            device_id=other_core,
            device_id_type=MESH,
        ).wait_recv()

    def hblk(q):
        return mb.at[q, c]

    def send_h(q, to, dev):
        send(hblk(q), hblk(q), to, dev)

    def send_section(q):
        for dx, dz in hier_offsets:
            hx, hz = hier(dx, dz)
            dev = (hx * 8 + hz, r)
            if q == 0:
                send(meta_out, meta_in.at[h], R_M + 8 * dx + dz, dev)
            send(sblk.at[hz, 2 * hx + q], zin[q].at[pl.ds(3 * h, 3)], R_A + 16 * q + 8 * dx + dz, dev)

    def send_columns(way):
        for dx, dy in row_offsets:
            if dx == way:
                q = chip(dx, dy)
                send(sblk.at[q], lb.at[p, c], R_L + 4 * dx + dy, (h, q * 2 + c))

    send_h(p, R_HN, x_cross)
    send_h(p, R_HU, rowdev(0, 1))
    send_h(p, R_HD, rowdev(0, 3))
    send_section(0)
    send_h(p, R_HP, other_core)

    q = chip(1, 0)
    arrived(hblk(q), R_HN)
    send_h(q, R_HU + 1, rowdev(0, 1))
    send_h(q, R_HD + 1, rowdev(0, 3))
    send_columns(1)
    send_section(1)
    send_h(q, R_HP + 4, other_core)
    send(sblk.at[p], lb.at[p, c], R_LP, other_core)
    lb[p, c] = sblk[p]
    for q in range(2):
        zin[q][pl.ds(3 * h, 3)] = sblk[z, 2 * xh + q]

    for copy in small[2:]:
        copy.wait()
    for k in range(MODES):
        line_v = cv[pl.ds(k, 1), pl.ds(pl.multiple_of(128 * p, 128), 128)]
        vt[k] = jnp.broadcast_to(line_v, (128, 128)).T
        v_rows = vt[k, pl.ds(pl.multiple_of(64 * c + 32 * xh, 32), 32), :]
        v_cols = cv[pl.ds(k, 1), pl.ds(pl.multiple_of(128 * z, 128), 128)]
        diff = v_rows - v_cols
        dk[k] = diff
        dg[k] = coup[0, k] * diff
        eg[k] = coup[1, k] * (v_rows + v_cols)

    def half_h(q, half):
        return mb.at[q, c, pl.ds(32 * half, 32)]

    for dx in range(2):
        below, above = chip(dx, 3), chip(dx, 1)
        arrived(hblk(below), R_HU + dx)
        send(half_h(below, 0), half_h(below, 0), R_H2 + 2 * dx, rowdev(0, 1))
        arrived(hblk(above), R_HD + dx)
        send(half_h(above, 1), half_h(above, 1), R_H2 + 2 * dx + 1, rowdev(0, 3))
        send_h(below, R_HP + 4 * dx + 3, other_core)
        send_h(above, R_HP + 4 * dx + 1, other_core)
    send_columns(0)
    for dx in range(2):
        q = chip(dx, 2)
        arrived(half_h(q, 0), R_H2 + 2 * dx)
        arrived(half_h(q, 1), R_H2 + 2 * dx + 1)
        send_h(q, R_HP + 4 * dx + 2, other_core)

    for dx, dz in hier_offsets:
        hx, hz = hier(dx, 8 - dz)
        arrived(meta_in.at[hx * 8 + hz], R_M + 8 * dx + dz)
    meta_v[...] = jnp.minimum(jnp.sum(meta_in[...], axis=0), ADOS - 1)
    cp_m = pltpu.make_async_copy(meta_v, meta_s, lsem.at[3])
    cp_m.start()
    cp_m.wait()

    def couple(q):
        for dx, dz in hier_offsets:
            hx, hz = hier(dx, 8 - dz)
            arrived(zin[q].at[pl.ds(3 * (hx * 8 + hz), 3)], R_A + 16 * q + 8 * dx + dz)
        rows = pl.ds(16 * q, 16)
        for place, entry in enumerate(TABLE):
            re = jnp.zeros((16, 128), F32)
            im = jnp.zeros((16, 128), F32)
            for k in range(MODES):
                child = shifted(entry, k, 1)
                if child is not None:
                    near = zin[q][meta_s[0, child]].astype(F32)
                    re = re + dk[k, rows] * near[1]
                    im = im - dk[k, rows] * near[0]
                if entry[k] > 0:
                    near = zin[q][meta_s[0, shifted(entry, k, -1)]].astype(F32)
                    add_re = dg[k, rows] * near[1] + eg[k, rows] * near[0]
                    add_im = eg[k, rows] * near[1] - dg[k, rows] * near[0]
                    if entry[k] > 1:
                        add_re = add_re * float(entry[k])
                        add_im = add_im * float(entry[k])
                    re = re + add_re
                    im = im + add_im
            ccan[place, 0] = re.astype(BF16)
            ccan[place, 1] = im.astype(BF16)
        for slot in range(ADOS):
            cout[q, slot] = ccan[meta_s[1, slot]]
        for dx, dz in hier_offsets:
            hx, hz = hier(dx, dz)
            to = hx * 8 + hz
            send(cout.at[q, pl.ds(3 * to, 3)], cret.at[2 * xh + q, z], R_C + 16 * q + 8 * dx + dz, (to, r))
        cret[2 * xh + q, z] = cout[q, pl.ds(3 * h, 3)]

    couple(0)

    for dx, dy in row_offsets:
        back = (4 - dy) % 4
        q = chip(dx, back)
        arrived(lb.at[q, c], R_L + 4 * dx + dy)
        send(lb.at[q, c], lb.at[q, c], R_LP + 4 * dx + back, other_core)

    for dx in range(2):
        for dy in range(4):
            arrived(mb.at[chip(dx, dy), oc], R_HP + 4 * dx + dy)
    under = lax.broadcasted_iota(jnp.int32, (128, 128), 0)
    along = lax.broadcasted_iota(jnp.int32, (128, 128), 1)

    def put(ri, i, j, tile):
        hn[ri, i, :, :, pl.ds(128 * j, 128)] = tile.reshape(2, 64, 128)

    for i in range(8):
        for j in range(i, 8):
            upper = mb[i, :, :, pl.ds(128 * j, 128)].reshape(128, 128)
            if i == j:
                wide = upper.astype(F32)
                flipped = wide.T
                put(0, i, i, jnp.where(along >= under, wide, flipped).astype(BF16))
                below = jnp.where(along > under, -flipped, 0.0)
                put(1, i, i, jnp.where(along < under, wide, below).astype(BF16))
            else:
                lower = mb[j, :, :, pl.ds(128 * i, 128)].reshape(128, 128)
                put(0, i, j, upper)
                put(0, j, i, upper.T)
                put(1, i, j, -lower.T)
                put(1, j, i, lower)


    couple(1)

    for dx in range(2):
        for dy in range(4):
            arrived(lb.at[chip(dx, dy), oc], R_LP + 4 * dx + dy)

    @pl.loop(0, 3)
    def _(a):
        real = lb[:, :, :, a, 0].reshape(N, 128)
        imag = lb[:, :, :, a, 1].reshape(N, 128)
        rhs = jnp.concatenate(
            [jnp.concatenate([real, imag], 1), jnp.concatenate([-imag, real], 1)], 0
        )
        for m in range(2):
            lhs = jnp.concatenate(
                [hn[ri, pl.ds(4 * m, 4), c].reshape(256, N) for ri in range(2)], 1
            )
            out = jnp.dot(lhs, rhs, preferred_element_type=F32).astype(BF16)
            out = out.reshape(4, 4, 16, 256)
            lout[pl.ds(4 * m, 4), :, a, 0] = out[..., :128]
            lout[pl.ds(4 * m, 4), :, a, 1] = out[..., 128:]

    for dx, dy in row_offsets:
        q = chip(dx, dy)
        send(lout.at[q], lret.at[p], R_LR + 4 * dx + dy, (h, q * 2 + c))
    lret[p] = lout[p]

    @pl.loop(0, 4)
    def _(n):
        cols = pl.ds(pl.multiple_of(256 * n, 256), 256)
        rhs = jnp.concatenate(
            [hn[ri, :, :, :, cols].reshape(N, 256) for ri in range(2)], 0
        )
        lhs = amat[...].reshape(384, 2 * N)
        out = jnp.dot(lhs, rhs, preferred_element_type=F32)
        rbuf[:, :, :, :, cols] = out.reshape(4, 3, 2, 16, 256)

    for q in range(2):
        for dx, dz in hier_offsets:
            hx, hz = hier(dx, 8 - dz)
            arrived(cret.at[2 * hx + q, hz], R_C + 16 * q + 8 * dx + dz)
    for dx, dy in row_offsets:
        back = (4 - dy) % 4
        arrived(lret.at[chip(dx, back)], R_LR + 4 * dx + dy)

    @pl.loop(0, 3)
    def _(a):
        decay = occ[a, 0].astype(F32) * damp[0]
        for k in range(1, MODES):
            decay = decay + occ[a, k].astype(F32) * damp[k]
        for quarter in range(4):
            for b in range(8):
                cols = pl.ds(128 * b, 128)
                for ri in range(2):
                    turned = lret[b, quarter, a, 1 - ri].astype(F32) - rbuf[quarter, a, 1 - ri, :, cols]
                    if ri:
                        turned = -turned
                    value = turned - decay * sblk[b, quarter, a, ri].astype(F32)
                    value = value + cret[quarter, b, a, ri].astype(F32)
                    rows = pl.ds(16 * quarter, 16)
                    slope[a, ri, rows, cols] = value
                    acc_out[a, ri, rows, cols] = acc_v[a, ri, rows, cols] + (STEP / 3.0) * value

    for copy in sent:
        copy.wait_send()


def leave(slope, acc, slope_out, acc_out, sem):
    copies = []
    for a in range(3):
        for ri in range(2):
            for src, dst in ((slope, slope_out), (acc, acc_out)):
                copies.append(pltpu.make_async_copy(src.at[a, ri], dst.at[a, ri], sem.at[len(copies)]))
                copies[-1].start()
    for copy in copies:
        copy.wait()


def shards(state, prev_slope, accumulated, hamiltonian, couple_v, coupling, damping, occupation, parents, children):
    vmem = pltpu.VMEM
    anywhere = pl.BlockSpec(memory_space=pl.ANY)
    in_vmem = pl.BlockSpec(memory_space=pltpu.VMEM)
    block = vmem((3, 2, 64, N), F32)
    results = pl.pallas_call(
        kernel,
        name="section",
        out_shape=(block, block),
        in_specs=[anywhere] * 9,
        out_specs=(in_vmem, in_vmem),
        scratch_shapes=[
            vmem((3, 2, 64, N), BF16),
            vmem((3, 2, 64, N), F32),
            vmem((3, 2, 64, N), F32),
            vmem((MODES, N), F32),
            vmem((8, 128), jnp.int32),
            pltpu.SMEM((2, MODES), F32),
            pltpu.SMEM((MODES,), F32),
            pltpu.SMEM((3, MODES), jnp.int32),
            vmem((8, 4, 3, 2, 16, 128), BF16),
            vmem((4, 3, 2, 16, 2 * N), BF16),
            vmem((2, 64, N), BF16),
            vmem((8, 2, 64, N), BF16),
            vmem((2, 8, 2, 64, N), BF16),
            vmem((8, 2, 4, 3, 2, 16, 128), BF16),
            vmem((8, 4, 3, 2, 16, 128), BF16),
            vmem((8, 4, 3, 2, 16, 128), BF16),
            vmem((ADOS, 2, 16, 128), BF16),
            vmem((ADOS, 2, 16, 128), BF16),
            vmem((ADOS, 2, 16, 128), BF16),
            vmem((2, ADOS, 2, 16, 128), BF16),
            vmem((4, 8, 3, 2, 16, 128), BF16),
            vmem((4, 3, 2, 16, N), F32),
            vmem((8, 128), jnp.int32),
            vmem((16, 8, 128), jnp.int32),
            vmem((8, 128), jnp.int32),
            pltpu.SMEM((8, 128), jnp.int32),
            vmem((MODES, 128, 128), F32),
            vmem((MODES, 32, 128), F32),
            vmem((MODES, 32, 128), F32),
            vmem((MODES, 32, 128), F32),
            pltpu.SemaphoreType.DMA((16,)),
            pltpu.SemaphoreType.DMA((N_SEND,)),
            pltpu.SemaphoreType.DMA((N_RECV,)),
        ],
        compiler_params=pltpu.CompilerParams(collective_id=0, has_side_effects=True),
    )(
        state,
        prev_slope,
        accumulated,
        hamiltonian,
        couple_v,
        coupling,
        damping,
        occupation,
        jnp.asarray(key_table()),
    )
    whole = jax.ShapeDtypeStruct((3, 2, 64, N), F32)
    return pl.pallas_call(
        leave,
        name="leave",
        out_shape=(whole, whole),
        in_specs=[in_vmem, in_vmem],
        out_specs=(anywhere, anywhere),
        scratch_shapes=[pltpu.SemaphoreType.DMA((12,))],
        compiler_params=pltpu.CompilerParams(vmem_limit_bytes=1 << 20),
    )(*results)


def solution(mesh):
    block = P("hier", None, "row", None)
    return jax.shard_map(
        shards,
        mesh=mesh,
        in_specs=(
            block,
            block,
            block,
            P(None, "row", None),
            P(),
            P(),
            P(),
            P("hier", None),
            P("hier", None),
            P("hier", None),
        ),
        out_specs=(block, block),
        check_vma=False,
    )
```

```python
import jax
import jax.numpy as jnp
import numpy as np
from jax import lax
from jax.experimental import pallas as pl
from jax.experimental.pallas import tpu as pltpu
from jax.sharding import PartitionSpec as P

MESH = pl.DeviceIdType.MESH
N = 1024
MODES = 6
ADOS = 48
STEP = 0.5
F32 = jnp.float32
BF16 = jnp.bfloat16


def window_table():
    entries = [()]
    for _ in range(MODES):
        entries = [entry + (level,) for entry in entries for level in range(5)]
    chosen = [entry for entry in entries if sum(entry) <= 4]
    return sorted(chosen, key=lambda entry: (sum(entry), entry))[:ADOS]


TABLE = window_table()
PLACE = {entry: place for place, entry in enumerate(TABLE)}


def key_of(entry):
    return sum(entry[k] * 5**k for k in range(MODES))


def shifted(entry, mode, by):
    return PLACE.get(entry[:mode] + (entry[mode] + by,) + entry[mode + 1 :])


def key_table():
    keys = np.full((8, 128), -1, np.int32)
    keys[:, :ADOS] = [key_of(entry) for entry in TABLE]
    return keys


R_HN = 0
R_HU = 1
R_HD = 3
R_H2 = 5
R_HP = 9
R_L = 17
R_LP = 25
R_M = 41
R_A = 57
R_C = 89
R_LR = 121
N_RECV = 145
N_SEND = 140


def kernel(
    state,
    prev,
    acc,
    ham,
    cv_in,
    coup_in,
    damp_in,
    occ_in,
    tab_in,
    slope,
    acc_out,
    st_v,
    pv_v,
    acc_v,
    cv,
    tab,
    coup,
    damp,
    occ,
    sblk,
    amat,
    hv,
    mb,
    hn,
    lb,
    lout,
    lret,
    zin_0,
    zin_1,
    ccan,
    cout,
    cret,
    rbuf,
    meta_out,
    meta_in,
    meta_v,
    meta_s,
    vt,
    dk,
    dg,
    eg,
    lsem,
    ssem,
    rsem,
):
    h = lax.axis_index("hier")
    r = lax.axis_index("row")
    xh, z = lax.div(h, 8), lax.rem(h, 8)
    p, c = lax.div(r, 2), lax.rem(r, 2)
    xl, y = lax.div(p, 4), lax.rem(p, 4)
    oc = 1 - c
    zin = (zin_0, zin_1)

    def chip(dx, dy):
        return lax.rem(xl + dx, 2) * 4 + lax.rem(y + dy, 4)

    def rowdev(dx, dy):
        return (h, chip(dx, dy) * 2 + c)

    def hier(dx, dz):
        return lax.rem(xh + dx, 2), lax.rem(z + dz, 8)

    other_core = (h, p * 2 + oc)
    x_cross = ((1 - xh) * 8 + z, ((1 - xl) * 4 + y) * 2 + c)

    row_offsets = [(dx, dy) for dy in (2, 1, 3, 0) for dx in (1, 0) if dx or dy]
    hier_offsets = [(dx, dz) for dz in (4, 3, 5, 2, 6, 1, 7, 0) for dx in (1, 0) if dx or dz]

    cp_h = pltpu.make_async_copy(ham, hv, lsem.at[0])
    cp_s = pltpu.make_async_copy(state, st_v, lsem.at[1])
    cp_p = pltpu.make_async_copy(prev, pv_v, lsem.at[2])
    cp_s.start()
    cp_p.start()
    cp_h.start()
    small = []
    for i, (src, dst) in enumerate(
        [(occ_in, occ), (tab_in, tab), (cv_in, cv), (coup_in, coup), (damp_in, damp), (acc, acc_v)]
    ):
        small.append(pltpu.make_async_copy(src, dst, lsem.at[10 + i]))
        small[i].start()

    barrier = pltpu.get_barrier_semaphore()
    greeted = []
    for dx, dz in hier_offsets:
        hx, hz = hier(dx, dz)
        greeted.append((hx * 8 + hz, r))
    greeted += [rowdev(dx, dy) for dx, dy in row_offsets]
    greeted += [x_cross, other_core]
    for dev in greeted:
        pl.semaphore_signal(barrier, inc=1, device_id=dev, device_id_type=MESH)

    for copy in small[:2]:
        copy.wait()
    lane = lax.broadcasted_iota(jnp.int32, (8, 128), 1)
    line = lax.broadcasted_iota(jnp.int32, (8, 128), 0)
    slots = jnp.zeros((8, 128), jnp.int32)
    places = jnp.zeros((8, 128), jnp.int32)
    for j in range(3):
        key = occ[j, 0]
        for k in range(1, MODES):
            key = key + occ[j, k] * (5**k)
        hit = tab[...] == key
        slots = slots + jnp.where(hit, 3 * h + j, 0)
        place = jnp.sum(jnp.where(hit, lane, 0), axis=1, keepdims=True)
        places = places + jnp.where(lane == 3 * h + j, place, 0)
    mine = jnp.where(line == 0, slots, places)
    meta_out[...] = mine
    meta_in[h] = mine

    cp_s.wait()
    cp_p.wait()

    @pl.loop(0, 3)
    def _(a):
        for quarter in range(4):
            rows = pl.ds(16 * quarter, 16)
            for b in range(8):
                cols = pl.ds(128 * b, 128)
                parts = []
                for ri in range(2):
                    value = st_v[a, ri, rows, cols].astype(F32) + (0.5 * STEP) * pv_v[a, ri, rows, cols]
                    parts.append(value.astype(BF16))
                    sblk[b, quarter, a, ri] = parts[ri]
                    amat[quarter, a, ri, :, cols] = parts[ri]
                late = pl.ds(N + 128 * b, 128)
                amat[quarter, a, 0, :, late] = -parts[1]
                amat[quarter, a, 1, :, late] = parts[0]

    cp_h.wait()
    across = lax.broadcasted_iota(jnp.int32, (64, N), 1)
    down = lax.broadcasted_iota(jnp.int32, (64, N), 0) + 64 * r
    mb[p, c] = jnp.where(across >= down, hv[0].astype(F32), hv[1].astype(F32)).astype(BF16)

    pl.semaphore_wait(barrier, len(greeted))

    sent = []

    def send(src, dst, to, dev):
        copy = pltpu.make_async_remote_copy(
            src_ref=src,
            dst_ref=dst,
            send_sem=ssem.at[len(sent)],
            recv_sem=rsem.at[to],
            device_id=dev,
            device_id_type=MESH,
        )
        copy.start()
        sent.append(copy)

    def arrived(dst, to):
        pltpu.make_async_remote_copy(
            src_ref=dst,
            dst_ref=dst,
            send_sem=ssem.at[0],
            recv_sem=rsem.at[to],
            device_id=other_core,
            device_id_type=MESH,
        ).wait_recv()

    def hblk(q):
        return mb.at[q, c]

    def send_h(q, to, dev):
        send(hblk(q), hblk(q), to, dev)

    def send_section(q):
        for dx, dz in hier_offsets:
            hx, hz = hier(dx, dz)
            dev = (hx * 8 + hz, r)
            if q == 0:
                send(meta_out, meta_in.at[h], R_M + 8 * dx + dz, dev)
            send(sblk.at[hz, 2 * hx + q], zin[q].at[pl.ds(3 * h, 3)], R_A + 16 * q + 8 * dx + dz, dev)

    def send_columns(way):
        for dx, dy in row_offsets:
            if dx == way:
                q = chip(dx, dy)
                send(sblk.at[q], lb.at[p, c], R_L + 4 * dx + dy, (h, q * 2 + c))

    send_h(p, R_HN, x_cross)
    send_h(p, R_HU, rowdev(0, 1))
    send_h(p, R_HD, rowdev(0, 3))
    send_section(0)
    send_h(p, R_HP, other_core)

    q = chip(1, 0)
    arrived(hblk(q), R_HN)
    send_h(q, R_HU + 1, rowdev(0, 1))
    send_h(q, R_HD + 1, rowdev(0, 3))
    send_columns(1)
    send_section(1)
    send_h(q, R_HP + 4, other_core)
    send(sblk.at[p], lb.at[p, c], R_LP, other_core)
    lb[p, c] = sblk[p]
    for q in range(2):
        zin[q][pl.ds(3 * h, 3)] = sblk[z, 2 * xh + q]

    for copy in small[2:]:
        copy.wait()
    for k in range(MODES):
        line_v = cv[pl.ds(k, 1), pl.ds(pl.multiple_of(128 * p, 128), 128)]
        vt[k] = jnp.broadcast_to(line_v, (128, 128)).T
        v_rows = vt[k, pl.ds(pl.multiple_of(64 * c + 32 * xh, 32), 32), :]
        v_cols = cv[pl.ds(k, 1), pl.ds(pl.multiple_of(128 * z, 128), 128)]
        diff = v_rows - v_cols
        dk[k] = diff
        dg[k] = coup[0, k] * diff
        eg[k] = coup[1, k] * (v_rows + v_cols)

    def half_h(q, half):
        return mb.at[q, c, pl.ds(32 * half, 32)]

    for dx in range(2):
        below, above = chip(dx, 3), chip(dx, 1)
        arrived(hblk(below), R_HU + dx)
        send(half_h(below, 0), half_h(below, 0), R_H2 + 2 * dx, rowdev(0, 1))
        arrived(hblk(above), R_HD + dx)
        send(half_h(above, 1), half_h(above, 1), R_H2 + 2 * dx + 1, rowdev(0, 3))
        send_h(below, R_HP + 4 * dx + 3, other_core)
        send_h(above, R_HP + 4 * dx + 1, other_core)
    send_columns(0)
    for dx in range(2):
        q = chip(dx, 2)
        arrived(half_h(q, 0), R_H2 + 2 * dx)
        arrived(half_h(q, 1), R_H2 + 2 * dx + 1)
        send_h(q, R_HP + 4 * dx + 2, other_core)

    for dx, dz in hier_offsets:
        hx, hz = hier(dx, 8 - dz)
        arrived(meta_in.at[hx * 8 + hz], R_M + 8 * dx + dz)
    meta_v[...] = jnp.minimum(jnp.sum(meta_in[...], axis=0), ADOS - 1)
    cp_m = pltpu.make_async_copy(meta_v, meta_s, lsem.at[3])
    cp_m.start()
    cp_m.wait()

    def couple(q):
        for dx, dz in hier_offsets:
            hx, hz = hier(dx, 8 - dz)
            arrived(zin[q].at[pl.ds(3 * (hx * 8 + hz), 3)], R_A + 16 * q + 8 * dx + dz)
        rows = pl.ds(16 * q, 16)
        for place, entry in enumerate(TABLE):
            re = jnp.zeros((16, 128), F32)
            im = jnp.zeros((16, 128), F32)
            for k in range(MODES):
                child = shifted(entry, k, 1)
                if child is not None:
                    near = zin[q][meta_s[0, child]].astype(F32)
                    re = re + dk[k, rows] * near[1]
                    im = im - dk[k, rows] * near[0]
                if entry[k] > 0:
                    near = zin[q][meta_s[0, shifted(entry, k, -1)]].astype(F32)
                    add_re = dg[k, rows] * near[1] + eg[k, rows] * near[0]
                    add_im = eg[k, rows] * near[1] - dg[k, rows] * near[0]
                    if entry[k] > 1:
                        add_re = add_re * float(entry[k])
                        add_im = add_im * float(entry[k])
                    re = re + add_re
                    im = im + add_im
            ccan[place, 0] = re.astype(BF16)
            ccan[place, 1] = im.astype(BF16)
        for slot in range(ADOS):
            cout[q, slot] = ccan[meta_s[1, slot]]
        for dx, dz in hier_offsets:
            hx, hz = hier(dx, dz)
            to = hx * 8 + hz
            send(cout.at[q, pl.ds(3 * to, 3)], cret.at[2 * xh + q, z], R_C + 16 * q + 8 * dx + dz, (to, r))
        cret[2 * xh + q, z] = cout[q, pl.ds(3 * h, 3)]

    couple(0)

    for dx, dy in row_offsets:
        back = (4 - dy) % 4
        q = chip(dx, back)
        arrived(lb.at[q, c], R_L + 4 * dx + dy)
        send(lb.at[q, c], lb.at[q, c], R_LP + 4 * dx + back, other_core)

    for dx in range(2):
        for dy in range(4):
            arrived(mb.at[chip(dx, dy), oc], R_HP + 4 * dx + dy)
    under = lax.broadcasted_iota(jnp.int32, (128, 128), 0)
    along = lax.broadcasted_iota(jnp.int32, (128, 128), 1)

    def put(ri, i, j, tile):
        hn[ri, i, :, :, pl.ds(128 * j, 128)] = tile.reshape(2, 64, 128)

    for i in range(8):
        for j in range(i, 8):
            upper = mb[i, :, :, pl.ds(128 * j, 128)].reshape(128, 128)
            if i == j:
                wide = upper.astype(F32)
                flipped = wide.T
                put(0, i, i, jnp.where(along >= under, wide, flipped).astype(BF16))
                below = jnp.where(along > under, -flipped, 0.0)
                put(1, i, i, jnp.where(along < under, wide, below).astype(BF16))
            else:
                lower = mb[j, :, :, pl.ds(128 * i, 128)].reshape(128, 128)
                put(0, i, j, upper)
                put(0, j, i, upper.T)
                put(1, i, j, -lower.T)
                put(1, j, i, lower)


    couple(1)

    for dx in range(2):
        for dy in range(4):
            arrived(lb.at[chip(dx, dy), oc], R_LP + 4 * dx + dy)

    for a in range(3):
        real = lb[:, :, :, a, 0].reshape(N, 128)
        imag = lb[:, :, :, a, 1].reshape(N, 128)
        rhs = jnp.concatenate(
            [jnp.concatenate([real, imag], 1), jnp.concatenate([-imag, real], 1)], 0
        )
        for m in range(2):
            lhs = jnp.concatenate(
                [hn[ri, pl.ds(4 * m, 4), c].reshape(256, N) for ri in range(2)], 1
            )
            out = jnp.dot(lhs, rhs, preferred_element_type=F32).astype(BF16)
            out = out.reshape(4, 4, 16, 256)
            lout[pl.ds(4 * m, 4), :, a, 0] = out[..., :128]
            lout[pl.ds(4 * m, 4), :, a, 1] = out[..., 128:]
        for dx, dy in row_offsets:
            q = chip(dx, dy)
            send(lout.at[q, :, a], lret.at[p, :, a], R_LR + 8 * a + 4 * dx + dy, (h, q * 2 + c))
    lret[p] = lout[p]

    @pl.loop(0, 4)
    def _(n):
        cols = pl.ds(pl.multiple_of(256 * n, 256), 256)
        rhs = jnp.concatenate(
            [hn[ri, :, :, :, cols].reshape(N, 256) for ri in range(2)], 0
        )
        lhs = amat[...].reshape(384, 2 * N)
        out = jnp.dot(lhs, rhs, preferred_element_type=F32)
        rbuf[:, :, :, :, cols] = out.reshape(4, 3, 2, 16, 256)

    for q in range(2):
        for dx, dz in hier_offsets:
            hx, hz = hier(dx, 8 - dz)
            arrived(cret.at[2 * hx + q, hz], R_C + 16 * q + 8 * dx + dz)
    for dx, dy in row_offsets:
        back = (4 - dy) % 4
        for a in range(3):
            arrived(lret.at[chip(dx, back), :, a], R_LR + 8 * a + 4 * dx + dy)

    @pl.loop(0, 3)
    def _(a):
        decay = occ[a, 0].astype(F32) * damp[0]
        for k in range(1, MODES):
            decay = decay + occ[a, k].astype(F32) * damp[k]
        for quarter in range(4):
            for b in range(8):
                cols = pl.ds(128 * b, 128)
                for ri in range(2):
                    turned = lret[b, quarter, a, 1 - ri].astype(F32) - rbuf[quarter, a, 1 - ri, :, cols]
                    if ri:
                        turned = -turned
                    value = turned - decay * sblk[b, quarter, a, ri].astype(F32)
                    value = value + cret[quarter, b, a, ri].astype(F32)
                    rows = pl.ds(16 * quarter, 16)
                    slope[a, ri, rows, cols] = value
                    acc_out[a, ri, rows, cols] = acc_v[a, ri, rows, cols] + (STEP / 3.0) * value

    for copy in sent:
        copy.wait_send()


def leave(slope, acc, slope_out, acc_out, sem):
    copies = []
    for a in range(3):
        for ri in range(2):
            for src, dst in ((slope, slope_out), (acc, acc_out)):
                copies.append(pltpu.make_async_copy(src.at[a, ri], dst.at[a, ri], sem.at[len(copies)]))
                copies[-1].start()
    for copy in copies:
        copy.wait()


def shards(state, prev_slope, accumulated, hamiltonian, couple_v, coupling, damping, occupation, parents, children):
    vmem = pltpu.VMEM
    anywhere = pl.BlockSpec(memory_space=pl.ANY)
    in_vmem = pl.BlockSpec(memory_space=pltpu.VMEM)
    block = vmem((3, 2, 64, N), F32)
    results = pl.pallas_call(
        kernel,
        name="section",
        out_shape=(block, block),
        in_specs=[anywhere] * 9,
        out_specs=(in_vmem, in_vmem),
        scratch_shapes=[
            vmem((3, 2, 64, N), BF16),
            vmem((3, 2, 64, N), F32),
            vmem((3, 2, 64, N), F32),
            vmem((MODES, N), F32),
            vmem((8, 128), jnp.int32),
            pltpu.SMEM((2, MODES), F32),
            pltpu.SMEM((MODES,), F32),
            pltpu.SMEM((3, MODES), jnp.int32),
            vmem((8, 4, 3, 2, 16, 128), BF16),
            vmem((4, 3, 2, 16, 2 * N), BF16),
            vmem((2, 64, N), BF16),
            vmem((8, 2, 64, N), BF16),
            vmem((2, 8, 2, 64, N), BF16),
            vmem((8, 2, 4, 3, 2, 16, 128), BF16),
            vmem((8, 4, 3, 2, 16, 128), BF16),
            vmem((8, 4, 3, 2, 16, 128), BF16),
            vmem((ADOS, 2, 16, 128), BF16),
            vmem((ADOS, 2, 16, 128), BF16),
            vmem((ADOS, 2, 16, 128), BF16),
            vmem((2, ADOS, 2, 16, 128), BF16),
            vmem((4, 8, 3, 2, 16, 128), BF16),
            vmem((4, 3, 2, 16, N), F32),
            vmem((8, 128), jnp.int32),
            vmem((16, 8, 128), jnp.int32),
            vmem((8, 128), jnp.int32),
            pltpu.SMEM((8, 128), jnp.int32),
            vmem((MODES, 128, 128), F32),
            vmem((MODES, 32, 128), F32),
            vmem((MODES, 32, 128), F32),
            vmem((MODES, 32, 128), F32),
            pltpu.SemaphoreType.DMA((16,)),
            pltpu.SemaphoreType.DMA((N_SEND,)),
            pltpu.SemaphoreType.DMA((N_RECV,)),
        ],
        compiler_params=pltpu.CompilerParams(collective_id=0, has_side_effects=True),
    )(
        state,
        prev_slope,
        accumulated,
        hamiltonian,
        couple_v,
        coupling,
        damping,
        occupation,
        jnp.asarray(key_table()),
    )
    whole = jax.ShapeDtypeStruct((3, 2, 64, N), F32)
    return pl.pallas_call(
        leave,
        name="leave",
        out_shape=(whole, whole),
        in_specs=[in_vmem, in_vmem],
        out_specs=(anywhere, anywhere),
        scratch_shapes=[pltpu.SemaphoreType.DMA((12,))],
        compiler_params=pltpu.CompilerParams(vmem_limit_bytes=1 << 20),
    )(*results)


def solution(mesh):
    block = P("hier", None, "row", None)
    return jax.shard_map(
        shards,
        mesh=mesh,
        in_specs=(
            block,
            block,
            block,
            P(None, "row", None),
            P(),
            P(),
            P(),
            P("hier", None),
            P("hier", None),
            P("hier", None),
        ),
        out_specs=(block, block),
        check_vma=False,
    )
```
